32 devices in a mesh: blk: 8 (over z, y), beam: 4 (over x, core).
Axes of the slice: x: 2, y: 2, z: 4, core: 2. Of those that a mesh axis runs over, the one named last changes fastest.
Arguments:
- signal: float32 [524288], P(('blk', 'beam')), may hold values from -6 to 6
- weight: float32 [524288], P(('blk', 'beam')), may hold values from 0.25 to 1
- cycle: int32 [524288], P(('blk', 'beam')), may hold values from 0 to 1
- phi: int32 [524288], P(('blk', 'beam')), may hold values from 0 to 2047
- psi: int32 [524288], P(('blk', 'beam')), may hold values from 0 to 31
- owner: int32 [4096, 1], P(('blk', 'beam')), may hold values from 0 to 7; in each aligned block of 128 rows (0 to 127, 128 to 255, ...) at most 40 rows name the same one
- wigner: bfloat16 [1024, 32, 16, 1152], P('blk', 'beam'), may hold values from -0.375 to 0.375
Outputs:
- alm: float32 [1024, 2, 1152], P(('blk', 'beam'))
The draws below stay inside these ranges and needn't reach their ends.
Inputs may be any that keep to these rules, and one draw needn't show every extreme that they name: `owner`: among the 128 blocks of one device no cycle group is named by more than 40 blocks, and in some device's blocks one group is named by exactly 40.
All inputs are finite; a program needn't handle non-finite values.
Results may differ from the reference program's by a relative error of at most 0.02.
Values may be sent and summed in bfloat16 or wider, within the bound.
No kernel may reach another device: no remote copies, remote signals or barrier semaphores. Data moves between devices by JAX's collectives and lax.ppermute only.
A program may use at most 128 MiB of HBM per device.

```python
import math
import jax
import jax.numpy as jnp
import numpy as np
from jax import lax

BLK_DEV = 128
BLOCK_ROWS = 128
CYCLE_DEV = 2
NPSI = 32
NPHI = 2048
L = 1152
CAP = 40
CYCLES = 16
NM = 1024
BLOCKS = 4096
SAMPLES = 524288
N_BLK = 8


def with_ends(values, stream_key, least, top_value):
    spot = [jax.random.randint(jax.random.fold_in(stream_key, axis), (), 0, length) for axis, length in enumerate(values.shape)]
    longest = values.shape.index(max(values.shape))
    beside = spot[:longest] + [(spot[longest] + 1) % values.shape[longest]] + spot[longest + 1:]
    return values.at[tuple(spot)].set(least).at[tuple(beside)].set(top_value)


def strengthened(array, key, source, target, shards_of, factor):
    owner, partner = [(jnp.arange(array.shape[position]) // (array.shape[position] // shards_of)).reshape([-1 if axis == position else 1 for axis in range(array.ndim)]) for position in (source, target)]
    chosen = jax.random.permutation(key, shards_of)[partner]
    strong = (owner == chosen) | (owner == (partner + shards_of // 2) % shards_of)
    return jnp.where(strong, factor * array, array)


def level_of(key, dims, shards, low, largest):
    loudness, own = 1.0, jax.random.fold_in(key, 6)
    for dim, parts in shards:
        draws = jnp.exp(jax.random.uniform(jax.random.fold_in(own, dim), (parts,), jnp.float32, low / len(shards), largest / len(shards)))
        loudness = loudness * jnp.repeat(draws, dims[dim] // parts).reshape([-1 if axis == dim else 1 for axis in range(len(dims))])
    return loudness


def deal_out(own_key, own, number, rows, count, top, limit, skew):
    ranking = jax.random.permutation(own_key, count)
    crowded, usual = shares(count, rows * top, limit, skew, True), shares(count, rows * top, limit, skew, False)
    places = jnp.arange(count)

    def named(tallies, rotation):
        used = int((tallies > 0).sum())
        fixed = max(1, used // 4)
        shifted = fixed + (places - fixed + rotation * (used - fixed)) % max(1, count - fixed)
        return jnp.zeros((count,), jnp.int32).at[ranking[jnp.where(places < fixed, places, shifted)]].set(jnp.asarray(tallies, jnp.int32))

    tallies = jnp.where(number % 4 == 0, named(crowded, number // 4), named(usual, number - number // 4 - 1))
    mixed = jax.random.permutation(jax.random.fold_in(own, 3), count)
    donor, sink = mixed[0:count // 2 * 2:2], mixed[1:count // 2 * 2:2]
    margin = jnp.minimum(tallies[donor] - 1, limit - tallies[sink]) // 2
    margin = jnp.where((donor == ranking[0]) | (sink == ranking[0]) | (tallies[sink] == 0), 0, jnp.maximum(margin, 0))
    shifted = jax.random.randint(jax.random.fold_in(own, 4), (count // 2,), 0, 1 << 20) % (margin + 1)
    tallies = tallies.at[donor].add(-shifted).at[sink].add(shifted)
    items = jnp.searchsorted(jnp.cumsum(tallies), jnp.arange(rows * top), side="right").astype(jnp.int32)
    table = items.reshape(top, rows).T
    table = table[jax.random.permutation(jax.random.fold_in(own, 1), rows)]
    rotation = jax.random.randint(jax.random.fold_in(own, 2), (rows, 1), 0, top)
    return jnp.take_along_axis(table, (jnp.arange(top)[None, :] + rotation) % top, axis=1)


def shares(number_of, total, bound, slope, full):
    loads = [(1 << 20) // math.isqrt(grade ** slope) + 1 for grade in range(1, number_of + 1)]
    largest = bound if full else min(bound, max(-(-total // number_of), total * loads[0] // sum(loads)))
    least = 1 if total - largest >= number_of - 1 else 0
    given, spare = [largest] + [least] * (number_of - 1), total - largest - least * (number_of - 1)
    while spare > 0:
        movable = [i for i in range(1, number_of) if given[i] < largest] or [i for i in range(1, number_of) if given[i] < bound]
        whole, left = sum([loads[i] for i in movable]), spare
        for i in movable:
            extra = min(bound - given[i], max(1, left * loads[i] // whole), spare)
            given[i] = given[i] + extra
            spare = spare - extra
    return np.array(given)


def gaussian(key, extent, width, reach, pieces=(), held_as=jnp.bfloat16):
    array = jax.random.normal(key, extent, jnp.float32) * width
    if len(pieces) > 0:
        array = level_of(key, extent, pieces, -0.22, 0.18) * array
    return jnp.clip(array, min=-reach, max=reach).astype(held_as)


def heavy_noise(rng, extent, width, most, split, heavy, kind=jnp.bfloat16):
    values = width * jax.random.normal(rng, extent, jnp.float32)
    if split:
        values = values * level_of(rng, extent, split, -0.22, 0.18)
    return jnp.clip(strengthened(values, jax.random.fold_in(rng, 3), *heavy), -most, most).astype(kind)


def setup_inputs(seed: int = 0) -> dict:
    key_list = jax.random.split(jax.random.key(seed), 8)
    signal = gaussian(key_list[0], (SAMPLES,), 1.0, 6.0, ((0, 32),), jnp.float32)
    weight = jnp.clip(0.25 + 0.75 * jax.random.uniform(key_list[1], (SAMPLES,), jnp.float32) ** level_of(key_list[1], (SAMPLES,), ((0, 32),), -0.2, 0.2), 0.25, 1.0)
    cycle = with_ends(jax.random.randint(key_list[2], (SAMPLES,), 0, CYCLE_DEV), jax.random.fold_in(key_list[2], 1), 0, CYCLE_DEV - 1).astype(jnp.int32)
    phi = with_ends(jax.random.randint(key_list[3], (SAMPLES,), 0, NPHI), jax.random.fold_in(key_list[3], 1), 0, NPHI - 1).astype(jnp.int32)
    psi = with_ends(jax.random.randint(key_list[4], (SAMPLES,), 0, NPSI), jax.random.fold_in(key_list[4], 1), 0, NPSI - 1).astype(jnp.int32)
    owner_keys = jax.random.split(jax.random.fold_in(key_list[5], 1), BLOCKS // BLK_DEV)
    owner_turns = jax.random.permutation(jax.random.fold_in(key_list[5], 3), BLOCKS // BLK_DEV)
    owner = jax.vmap(lambda own, number: deal_out(jax.random.fold_in(key_list[5], 2), own, number, BLK_DEV, N_BLK, 1, CAP, 2))(owner_keys, owner_turns).reshape((BLOCKS, 1))
    wigner = heavy_noise(key_list[6], (NM, NPSI, CYCLES, L), (NPSI * CYCLES) ** -0.5, 0.375, ((0, 8), (1, 4)), (1, 0, 8, 2.0))
    return {"signal": signal, "weight": weight, "cycle": cycle, "phi": phi, "psi": psi, "owner": owner, "wigner": wigner}


def psi_rows(psi_index, length):
    component = jnp.arange(length, dtype=jnp.int32)[:, None]
    middle = length // 2
    frequency = jnp.where(component <= middle, component, component - middle)
    residue = (frequency * psi_index[None, :] % length).astype(jnp.float32)
    angles = residue * jnp.float32(2.0 * math.pi / length)
    return jnp.where(component <= middle, jnp.cos(angles), jnp.sin(angles)) * jnp.float32(1.0 / math.sqrt(length))

def phi_table(length):
    cell_index = jnp.arange(length, dtype=jnp.int32)[:, None]
    column = jnp.arange(length, dtype=jnp.int32)[None, :]
    residue = (column // 2 * cell_index % length).astype(jnp.float32)
    angles = residue * jnp.float32(2.0 * math.pi / length)
    values = jnp.where(column % 2 == 0, jnp.cos(angles), jnp.sin(angles)) * jnp.float32(1.0 / math.sqrt(length))
    return values.astype(jnp.bfloat16)

def reference(signal, weight, cycle, phi, psi, owner, wigner):
    sample_value = signal * weight
    beam_rows = psi_rows(psi, NPSI) * sample_value[None, :]
    beam_rows = lax.optimization_barrier(beam_rows.astype(jnp.bfloat16)).astype(jnp.float32)
    theta = jnp.repeat(owner[:, 0], BLOCK_ROWS) * CYCLE_DEV + cycle
    target = (theta * NPHI + phi).astype(jnp.int32)
    cube = jax.ops.segment_sum(beam_rows.T, target, num_segments=CYCLES * NPHI)
    cube = cube.reshape(CYCLES, NPHI, NPSI).transpose(0, 2, 1).astype(jnp.bfloat16)
    spectra = jnp.dot(cube.reshape(CYCLES * NPSI, NPHI), phi_table(NPHI), preferred_element_type=jnp.float32)
    spectra = spectra.astype(jnp.bfloat16).reshape(CYCLES, NPSI, NM, 2)
    stacked = spectra.transpose(2, 1, 0, 3).reshape(NM, NPSI * CYCLES, 2)

    def one_order(pair):
        table, column = pair
        return jnp.dot(column.T, table.reshape(NPSI * CYCLES, L), preferred_element_type=jnp.float32)
    return lax.map(one_order, (wigner, stacked))
```

```python
import math

import jax
import jax.numpy as jnp
import numpy as np
from jax import lax
from jax.experimental import pallas as pl
from jax.experimental.pallas import tpu as pltpu
from jax.sharding import PartitionSpec as P

BLOCK_ROWS = 128
CYCLE_DEV = 2
NPSI = 32
NPHI = 2048
LOW = 256
HIGH = NPHI // LOW
HALF = HIGH // 2
LANES = 128
F32 = jnp.float32
BF16 = jnp.bfloat16


def round_up(value, step):
    return -(-value // step) * step


def psi_matrix():
    component = np.arange(NPSI)[:, None]
    cell = np.arange(NPSI)[None, :]
    middle = NPSI // 2
    frequency = np.where(component <= middle, component, component - middle)
    angles = (frequency * cell % NPSI) * (2.0 * math.pi / NPSI)
    return np.where(component <= middle, np.cos(angles), np.sin(angles)) / math.sqrt(NPSI)


def first_matrix():
    psi = psi_matrix()
    out = np.zeros((2, HALF, NPSI, NPSI, HIGH))
    for parity in range(2):
        for a in range(HIGH):
            sign = -1.0 if parity == 1 and a >= HALF else 1.0
            out[parity, a % HALF, :, :, a] = sign * psi
    return out.reshape(2 * HALF * NPSI, NPSI * HIGH)


def second_tables(groups):
    orders = NPHI // 2 // groups
    width = round_up(orders, LANES)
    f = np.arange(NPHI // 2)
    out = np.zeros((2, NPHI // 2, groups, width))
    for parity in range(2):
        k = np.arange(orders // 2)
        m = np.arange(groups)[:, None] * orders + 2 * k[None, :] + parity
        angles = (f[:, None, None] * m[None] % NPHI) * (2.0 * math.pi / NPHI)
        out[parity, :, :, 0:orders:2] = np.cos(angles)
        out[parity, :, :, 1:orders:2] = np.sin(angles)
    out = out / math.sqrt(NPHI)
    return out.reshape(2, NPHI // 2, groups * width), width


def dot(a, b, ca, cb):
    return lax.dot_general(a, b, (((ca,), (cb,)), ((), ())), preferred_element_type=F32)


def pack_kernel(groups, cap, owner_ref, signal_ref, weight_ref, cycle_ref, phi_ref, psi_ref, out_ref):
    blocks = owner_ref.shape[1]
    padded = out_ref.shape[2]
    owner = owner_ref[...]
    rows = round_up(groups, 8)
    hits = (owner == lax.broadcasted_iota(jnp.int32, (rows, blocks), 0)).astype(F32)
    before = (
        lax.broadcasted_iota(jnp.int32, (blocks, blocks), 0)
        < lax.broadcasted_iota(jnp.int32, (blocks, blocks), 1)
    ).astype(F32)
    earlier = dot(hits.astype(BF16), before.astype(BF16), 1, 0)
    within = jnp.sum(earlier * hits, axis=0, keepdims=True)
    position = owner * padded + within.astype(jnp.int32)
    spread = (
        (position == lax.broadcasted_iota(jnp.int32, (groups * padded, blocks), 0))
        .astype(F32)
        .astype(BF16)
    )
    value = (signal_ref[...] * weight_ref[...]).astype(BF16)
    phi = phi_ref[...]
    high = (psi_ref[...] * HIGH + phi // LOW).astype(F32).astype(BF16)
    low = phi % LOW + 1
    low = jnp.where(cycle_ref[...] == 0, low, -low).astype(F32).astype(BF16)
    for number, plane in enumerate((value, high, low)):
        moved = dot(spread, plane, 1, 0).astype(BF16)
        for group in range(groups):
            out_ref[group, number] = moved[group * padded : (group + 1) * padded]


def bin_kernel(share, step, recv_ref, first_ref, second_ref, out_ref, acc_ref, table_ref, sem):
    groups, _, padded, _ = recv_ref.shape
    width = out_ref.shape[-1]
    copy = pltpu.make_async_copy(second_ref, table_ref, sem)
    copy.start()
    acc_ref[...] = jnp.zeros_like(acc_ref)
    places = lax.broadcasted_iota(jnp.int32, (LOW, LANES), 0).astype(F32)
    places_hi = places.astype(BF16)
    places_lo = (places + 1.0).astype(BF16)
    zero = jnp.zeros((LOW, LANES), BF16)
    one = jnp.ones((LOW, LANES), BF16)

    def one_source(source, carry):
        for start in range(0, padded, step):
            value = recv_ref[source, 0, start : start + step, :]
            high = recv_ref[source, 1, start : start + step, :]
            low = recv_ref[source, 2, start : start + step, :]
            parts = [[], [], []]
            blank = jnp.zeros_like(value)
            value0 = jnp.where(low > 0, value, blank)
            value1 = jnp.where(low > 0, blank, value)
            low = jnp.abs(low)
            for row in range(step):
                same = places_hi == high[row : row + 1, :]
                parts[0].append(jnp.where(same, value0[row : row + 1, :], zero))
                parts[1].append(jnp.where(same, value1[row : row + 1, :], zero))
                parts[2].append(jnp.where(places_lo == low[row : row + 1, :], one, zero))
            left0 = jnp.concatenate(parts[0], axis=1)
            left1 = jnp.concatenate(parts[1], axis=1)
            right = jnp.concatenate(parts[2], axis=1)
            acc_ref[0] += dot(left0, right, 1, 1)
            acc_ref[1] += dot(left1, right, 1, 1)
        return carry

    lax.fori_loop(0, groups, one_source, 0)
    first = first_ref[...]
    mixed = [dot(first, acc_ref[t].astype(BF16), 1, 0).astype(BF16) for t in range(CYCLE_DEV)]
    copy.wait()
    for parity in range(2):
        total = None
        for a0 in range(HALF):
            base = (parity * HALF + a0) * NPSI
            left = jnp.concatenate([part[base : base + NPSI] for part in mixed], axis=0)
            term = dot(left, table_ref[parity, a0 * LOW : (a0 + 1) * LOW, :], 1, 0)
            total = term if total is None else total + term
        total = total.astype(BF16)
        for group in range(groups):
            for beam in range(NPSI // share):
                for t in range(CYCLE_DEV):
                    base = t * NPSI + beam * share
                    out_ref[group, beam, parity, t] = total[
                        base : base + share, group * width : (group + 1) * width
                    ]


def coeff_kernel(groups, orders, recv_ref, out_ref):
    _, beams, _, cycles, share, width = recv_ref.shape
    thetas = groups * cycles
    depth = thetas * share
    row = lax.broadcasted_iota(jnp.int32, (depth, depth), 0)
    column = lax.broadcasted_iota(jnp.int32, (depth, depth), 1)
    swap = ((row % share) * thetas + row // share == column).astype(F32).astype(BF16)
    total = None
    for parity in range(2):
        parts = []
        for group in range(groups):
            for t in range(cycles):
                piece = recv_ref[group, 0, parity, t].astype(F32)
                for beam in range(1, beams):
                    piece = piece + recv_ref[group, beam, parity, t].astype(F32)
                parts.append(piece)
        stacked = jnp.concatenate(parts, axis=0).astype(BF16)
        turned = dot(stacked, swap, 0, 0).astype(BF16)
        row = lax.broadcasted_iota(jnp.int32, (2 * orders, width), 0)
        column = lax.broadcasted_iota(jnp.int32, (2 * orders, width), 1)
        place = (row // 4 * 2 + row % 2 == column) & (row // 2 % 2 == parity)
        term = dot(place.astype(F32).astype(BF16), turned, 1, 0)
        total = term if total is None else total + term
    out_ref[...] = total.astype(BF16)


def order_kernel(chunk, where_ref, coeff_ref, wigner_ref, out_ref):
    depth = coeff_ref.shape[1]
    coeff = coeff_ref[...]
    wide = jnp.concatenate([coeff] * chunk, axis=1)
    row = lax.broadcasted_iota(jnp.int32, wide.shape, 0) // 2
    column = lax.broadcasted_iota(jnp.int32, wide.shape, 1) // depth
    wide = jnp.where(row == column, wide.astype(F32), 0.0).astype(BF16)
    out_ref[...] = dot(wide, wigner_ref[...], 1, 0).astype(out_ref.dtype)


def shards(signal, weight, cycle, phi, psi, owner, wigner):
    groups = lax.axis_size("blk")
    beams = lax.axis_size("beam")
    blocks = owner.shape[0]
    cap = max(2, 5 * blocks // (2 * groups))
    padded = round_up(cap, 8)
    share = NPSI // beams
    orders = wigner.shape[0]
    ells = wigner.shape[3]
    depth = share * groups * CYCLE_DEV

    def square(data):
        return data.reshape(blocks, BLOCK_ROWS)

    sent = pl.pallas_call(
        lambda *refs: pack_kernel(groups, cap, *refs),
        out_shape=jax.ShapeDtypeStruct((groups, 3, padded, BLOCK_ROWS), BF16),
        name="pack",
    )(owner.reshape(1, blocks), square(signal), square(weight), square(cycle), square(phi), square(psi))
    got = lax.all_to_all(sent, "blk", split_axis=0, concat_axis=0, tiled=True)
    tables, width = second_tables(groups)
    whole = pl.BlockSpec(memory_space=pltpu.VMEM)
    spectra = pl.pallas_call(
        lambda *refs: bin_kernel(share, 8, *refs),
        out_shape=jax.ShapeDtypeStruct((groups, beams, 2, CYCLE_DEV, share, width), BF16),
        in_specs=[whole, whole, pl.BlockSpec(memory_space=pl.ANY)],
        scratch_shapes=[
            pltpu.VMEM((CYCLE_DEV, LOW, LOW), F32),
            pltpu.VMEM(tables.shape, BF16),
            pltpu.SemaphoreType.DMA,
        ],
        name="bin",
    )(got, jnp.asarray(first_matrix(), BF16), jnp.asarray(tables, BF16))
    rows = 2 * CYCLE_DEV * share
    spectra = spectra.reshape(groups * beams, rows, width)
    parts = lax.all_to_all(spectra, ("blk", "beam"), split_axis=0, concat_axis=0, tiled=True)
    parts = parts.reshape(groups, beams, 2, CYCLE_DEV, share, width)
    coeff = pl.pallas_call(
        lambda *refs: coeff_kernel(groups, orders, *refs),
        out_shape=jax.ShapeDtypeStruct((2 * orders, depth), BF16),
        name="coeff",
    )(parts)

    me = lax.axis_index("beam").astype(jnp.int32)
    flat = wigner.reshape(orders * depth, ells)
    mine = orders // beams
    chunk = 8
    steps = mine // chunk

    def piece(offset, kind):
        target = (me ^ offset).reshape(1)
        return pl.pallas_call(
            lambda *refs: order_kernel(chunk, *refs),
            out_shape=jax.ShapeDtypeStruct((2 * mine, ells), kind),
            grid_spec=pltpu.PrefetchScalarGridSpec(
                num_scalar_prefetch=1,
                grid=(steps,),
                in_specs=[
                    pl.BlockSpec((2 * chunk, depth), lambda i, at: (at[0] * steps + i, 0)),
                    pl.BlockSpec((chunk * depth, ells), lambda i, at: (at[0] * steps + i, 0)),
                ],
                out_specs=pl.BlockSpec((2 * chunk, ells), lambda i, at: (i, 0)),
            ),
            name="order",
        )(target, coeff, flat)

    total = None
    for offset in range(beams - 1, -1, -1):
        part = piece(offset, BF16 if offset else F32)
        if offset:
            part = lax.ppermute(part, "beam", [(i, i ^ offset) for i in range(beams)])
        part = part.astype(F32)
        total = part if total is None else total + part
    return total.reshape(mine, 2, ells)


def solution(mesh):
    return jax.shard_map(
        shards,
        mesh=mesh,
        in_specs=(
            P(("blk", "beam")),
            P(("blk", "beam")),
            P(("blk", "beam")),
            P(("blk", "beam")),
            P(("blk", "beam")),
            P(("blk", "beam"), None),
            P("blk", "beam", None, None),
        ),
        out_specs=P(("blk", "beam"), None, None),
        check_vma=False,
    )
```

```python
import math

import jax
import jax.numpy as jnp
import numpy as np
from jax import lax
from jax.experimental import pallas as pl
from jax.experimental.pallas import tpu as pltpu
from jax.sharding import PartitionSpec as P

BLOCK_ROWS = 128
CYCLE_DEV = 2
NPSI = 32
NPHI = 2048
LOW = 256
HIGH = NPHI // LOW
HALF = HIGH // 2
LANES = 128
F32 = jnp.float32
BF16 = jnp.bfloat16


def round_up(value, step):
    return -(-value // step) * step


def psi_matrix():
    component = np.arange(NPSI)[:, None]
    cell = np.arange(NPSI)[None, :]
    middle = NPSI // 2
    frequency = np.where(component <= middle, component, component - middle)
    angles = (frequency * cell % NPSI) * (2.0 * math.pi / NPSI)
    return np.where(component <= middle, np.cos(angles), np.sin(angles)) / math.sqrt(NPSI)


def first_matrix():
    psi = psi_matrix()
    out = np.zeros((2, HALF, NPSI, NPSI, HIGH))
    for parity in range(2):
        for a in range(HIGH):
            sign = -1.0 if parity == 1 and a >= HALF else 1.0
            out[parity, a % HALF, :, :, a] = sign * psi
    return out.reshape(2 * HALF * NPSI, NPSI * HIGH)


def second_tables(groups):
    orders = NPHI // 2 // groups
    width = round_up(orders, LANES)
    f = np.arange(NPHI // 2)
    out = np.zeros((2, NPHI // 2, groups, width))
    for parity in range(2):
        k = np.arange(orders // 2)
        m = np.arange(groups)[:, None] * orders + 2 * k[None, :] + parity
        angles = (f[:, None, None] * m[None] % NPHI) * (2.0 * math.pi / NPHI)
        out[parity, :, :, 0:orders:2] = np.cos(angles)
        out[parity, :, :, 1:orders:2] = np.sin(angles)
    out = out / math.sqrt(NPHI)
    return out.reshape(2, NPHI // 2, groups * width), width


def dot(a, b, ca, cb):
    return lax.dot_general(a, b, (((ca,), (cb,)), ((), ())), preferred_element_type=F32)


def pack_kernel(groups, me_ref, owner_ref, signal_ref, weight_ref, cycle_ref, phi_ref, psi_ref, out_ref, targets_ref):
    for offset in range(targets_ref.shape[0]):
        targets_ref[offset] = me_ref[0] ^ offset
    blocks = owner_ref.shape[1]
    padded = out_ref.shape[2]
    owner = owner_ref[...]
    rows = round_up(groups, 8)
    hits = (owner == lax.broadcasted_iota(jnp.int32, (rows, blocks), 0)).astype(F32)
    before = (
        lax.broadcasted_iota(jnp.int32, (blocks, blocks), 0)
        < lax.broadcasted_iota(jnp.int32, (blocks, blocks), 1)
    ).astype(F32)
    earlier = dot(hits.astype(BF16), before.astype(BF16), 1, 0)
    within = jnp.sum(earlier * hits, axis=0, keepdims=True)
    position = owner * padded + within.astype(jnp.int32)
    spread = (
        (position == lax.broadcasted_iota(jnp.int32, (groups * padded, blocks), 0))
        .astype(F32)
        .astype(BF16)
    )
    value = (signal_ref[...] * weight_ref[...]).astype(BF16)
    phi = phi_ref[...]
    high = (psi_ref[...] * HIGH + phi // LOW).astype(F32).astype(BF16)
    low = phi % LOW + 1
    low = jnp.where(cycle_ref[...] == 0, low, -low).astype(F32).astype(BF16)
    for number, plane in enumerate((value, high, low)):
        moved = dot(spread, plane, 1, 0).astype(BF16)
        for group in range(groups):
            out_ref[group, number] = moved[group * padded : (group + 1) * padded]


def bin_kernel(share, step, targets_ref, recv_ref, first_ref, second_ref, wigner_ref, out_ref, *rest):
    *held_refs, acc_ref, table_ref, sem, held_sem = rest
    groups, _, padded, _ = recv_ref.shape
    width = out_ref.shape[-1]
    copy = pltpu.make_async_copy(second_ref, table_ref, sem)
    copy.start()
    held = []
    size = held_refs[0].shape[0]
    for offset, held_ref in enumerate(held_refs):
        source = wigner_ref.at[pl.ds(targets_ref[offset] * size, size), :]
        held.append(pltpu.make_async_copy(source, held_ref, held_sem.at[offset]))
        held[-1].start()
    acc_ref[...] = jnp.zeros_like(acc_ref)
    places = lax.broadcasted_iota(jnp.int32, (LOW, LANES), 0).astype(F32)
    places_hi = places.astype(BF16)
    places_lo = (places + 1.0).astype(BF16)
    zero = jnp.zeros((LOW, LANES), BF16)
    one = jnp.ones((LOW, LANES), BF16)

    def one_source(source, carry):
        for start in range(0, padded, step):
            value = recv_ref[source, 0, start : start + step, :]
            high = recv_ref[source, 1, start : start + step, :]
            low = recv_ref[source, 2, start : start + step, :]
            parts = [[], [], []]
            blank = jnp.zeros_like(value)
            value0 = jnp.where(low > 0, value, blank)
            value1 = jnp.where(low > 0, blank, value)
            low = jnp.abs(low)
            for row in range(step):
                same = places_hi == high[row : row + 1, :]
                parts[0].append(jnp.where(same, value0[row : row + 1, :], zero))
                parts[1].append(jnp.where(same, value1[row : row + 1, :], zero))
                parts[2].append(jnp.where(places_lo == low[row : row + 1, :], one, zero))
            left0 = jnp.concatenate(parts[0], axis=1)
            left1 = jnp.concatenate(parts[1], axis=1)
            right = jnp.concatenate(parts[2], axis=1)
            acc_ref[0] += dot(left0, right, 1, 1)
            acc_ref[1] += dot(left1, right, 1, 1)
        return carry

    lax.fori_loop(0, groups, one_source, 0)
    first = first_ref[...]
    mixed = [dot(first, acc_ref[t].astype(BF16), 1, 0).astype(BF16) for t in range(CYCLE_DEV)]
    copy.wait()
    for parity in range(2):
        total = None
        for a0 in range(HALF):
            base = (parity * HALF + a0) * NPSI
            left = jnp.concatenate([part[base : base + NPSI] for part in mixed], axis=0)
            term = dot(left, table_ref[parity, a0 * LOW : (a0 + 1) * LOW, :], 1, 0)
            total = term if total is None else total + term
        total = total.astype(BF16)
        for group in range(groups):
            for beam in range(NPSI // share):
                for t in range(CYCLE_DEV):
                    base = t * NPSI + beam * share
                    out_ref[group, beam, parity, t] = total[
                        base : base + share, group * width : (group + 1) * width
                    ]
    for one in held:
        one.wait()


def coeff_kernel(groups, orders, recv_ref, out_ref):
    _, beams, _, cycles, share, width = recv_ref.shape
    thetas = groups * cycles
    depth = thetas * share
    row = lax.broadcasted_iota(jnp.int32, (depth, depth), 0)
    column = lax.broadcasted_iota(jnp.int32, (depth, depth), 1)
    swap = ((row % share) * thetas + row // share == column).astype(F32).astype(BF16)
    total = None
    for parity in range(2):
        parts = []
        for group in range(groups):
            for t in range(cycles):
                piece = recv_ref[group, 0, parity, t].astype(F32)
                for beam in range(1, beams):
                    piece = piece + recv_ref[group, beam, parity, t].astype(F32)
                parts.append(piece)
        stacked = jnp.concatenate(parts, axis=0).astype(BF16)
        turned = dot(stacked, swap, 0, 0).astype(BF16)
        row = lax.broadcasted_iota(jnp.int32, (2 * orders, width), 0)
        column = lax.broadcasted_iota(jnp.int32, (2 * orders, width), 1)
        place = (row // 4 * 2 + row % 2 == column) & (row // 2 % 2 == parity)
        term = dot(place.astype(F32).astype(BF16), turned, 1, 0)
        total = term if total is None else total + term
    out_ref[...] = total.astype(BF16)


def order_kernel(chunk, offset, where_ref, coeff_ref, wigner_ref, out_ref):
    depth = coeff_ref.shape[1]
    step = pl.program_id(0)
    coeff = coeff_ref[...]
    wide = jnp.concatenate([coeff] * chunk, axis=1)
    row = lax.broadcasted_iota(jnp.int32, wide.shape, 0) // 2
    column = lax.broadcasted_iota(jnp.int32, wide.shape, 1) // depth
    wide = jnp.where(row == column, wide.astype(F32), 0.0).astype(BF16)
    out_ref[...] = dot(wide, wigner_ref[pl.ds(step * chunk * depth, chunk * depth), :], 1, 0).astype(out_ref.dtype)


def shards(signal, weight, cycle, phi, psi, owner, wigner):
    groups = lax.axis_size("blk")
    beams = lax.axis_size("beam")
    blocks = owner.shape[0]
    cap = max(2, 5 * blocks // (2 * groups))
    padded = round_up(cap, 8)
    share = NPSI // beams
    orders = wigner.shape[0]
    ells = wigner.shape[3]
    depth = share * groups * CYCLE_DEV

    def square(data):
        return data.reshape(blocks, BLOCK_ROWS)

    whole = pl.BlockSpec(memory_space=pltpu.VMEM)
    me = lax.axis_index("beam").astype(jnp.int32)
    sent, targets = pl.pallas_call(
        lambda *refs: pack_kernel(groups, *refs),
        out_shape=(
            jax.ShapeDtypeStruct((groups, 3, padded, BLOCK_ROWS), BF16),
            jax.ShapeDtypeStruct((beams,), jnp.int32),
        ),
        in_specs=[pl.BlockSpec(memory_space=pltpu.SMEM)] + [whole] * 6,
        out_specs=(whole, pl.BlockSpec(memory_space=pltpu.SMEM)),
        compiler_params=pltpu.CompilerParams(vmem_limit_bytes=6 << 20),
        name="pack",
    )(me.reshape(1), owner.reshape(1, blocks), square(signal), square(weight), square(cycle), square(phi), square(psi))
    got = lax.all_to_all(sent, "blk", split_axis=0, concat_axis=0, tiled=True)
    tables, width = second_tables(groups)
    flat = wigner.reshape(orders * depth, ells)
    spectra, *held = pl.pallas_call(
        lambda *refs: bin_kernel(share, 8, *refs),
        out_shape=(
            jax.ShapeDtypeStruct((groups, beams, 2, CYCLE_DEV, share, width), BF16),
        )
        + tuple(pltpu.VMEM((flat.shape[0] // beams, ells), BF16) for _ in range(beams)),
        in_specs=[
            pl.BlockSpec(memory_space=pltpu.SMEM),
            whole,
            whole,
            pl.BlockSpec(memory_space=pltpu.HBM),
            pl.BlockSpec(memory_space=pl.ANY),
        ],
        out_specs=(whole,) * (1 + beams),
        scratch_shapes=[
            pltpu.VMEM((CYCLE_DEV, LOW, LOW), F32),
            pltpu.VMEM(tables.shape, BF16),
            pltpu.SemaphoreType.DMA,
            pltpu.SemaphoreType.DMA((beams,)),
        ],
        compiler_params=pltpu.CompilerParams(vmem_limit_bytes=2 * tables.size + (4 << 20)),
        name="bin",
    )(targets, got, jnp.asarray(first_matrix(), BF16), pltpu.with_memory_space_constraint(jnp.asarray(tables, BF16), pltpu.HBM), flat)
    rows = 2 * CYCLE_DEV * share
    spectra = spectra.reshape(groups * beams, rows, width)
    parts = lax.all_to_all(spectra, ("blk", "beam"), split_axis=0, concat_axis=0, tiled=True)
    parts = parts.reshape(groups, beams, 2, CYCLE_DEV, share, width)
    coeff = pl.pallas_call(
        lambda *refs: coeff_kernel(groups, orders, *refs),
        out_shape=jax.ShapeDtypeStruct((2 * orders, depth), BF16),
        compiler_params=pltpu.CompilerParams(vmem_limit_bytes=6 << 20),
        name="coeff",
    )(parts)

    mine = orders // beams
    chunk = 8
    steps = mine // chunk

    def piece(offset, kind):
        return pl.pallas_call(
            lambda *refs: order_kernel(chunk, offset, *refs),
            out_shape=jax.ShapeDtypeStruct((2 * mine, ells), kind),
            grid_spec=pltpu.PrefetchScalarGridSpec(
                num_scalar_prefetch=1,
                grid=(steps,),
                in_specs=[
                    pl.BlockSpec((2 * chunk, depth), lambda i, at: (at[offset] * steps + i, 0)),
                    pl.BlockSpec(memory_space=pltpu.VMEM),
                ],
                out_specs=pl.BlockSpec((2 * chunk, ells), lambda i, at: (i, 0)),
            ),
            compiler_params=pltpu.CompilerParams(vmem_limit_bytes=6 << 20),
            name="order",
        )(targets, coeff, pltpu.with_memory_space_constraint(held[offset], pltpu.VMEM))

    total = None
    for offset in range(beams - 1, -1, -1):
        part = piece(offset, BF16 if offset else F32)
        if offset:
            part = lax.ppermute(part, "beam", [(i, i ^ offset) for i in range(beams)])
        part = part.astype(F32)
        total = part if total is None else total + part
    return total.reshape(mine, 2, ells)


def solution(mesh):
    return jax.shard_map(
        shards,
        mesh=mesh,
        in_specs=(
            P(("blk", "beam")),
            P(("blk", "beam")),
            P(("blk", "beam")),
            P(("blk", "beam")),
            P(("blk", "beam")),
            P(("blk", "beam"), None),
            P("blk", "beam", None, None),
        ),
        out_specs=P(("blk", "beam"), None, None),
        check_vma=False,
    )
```

```python
import math

import jax
import jax.numpy as jnp
import numpy as np
from jax import lax
from jax.experimental import pallas as pl
from jax.experimental.pallas import tpu as pltpu
from jax.sharding import PartitionSpec as P


BLOCK_ROWS = 128
CYCLE_DEV = 2
NPSI = 32
NPHI = 2048
LOW = 256
HIGH = NPHI // LOW
HALF = HIGH // 2
LANES = 128
F32 = jnp.float32
BF16 = jnp.bfloat16


def round_up(value, step):
    return -(-value // step) * step


def psi_matrix():
    component = np.arange(NPSI)[:, None]
    cell = np.arange(NPSI)[None, :]
    middle = NPSI // 2
    frequency = np.where(component <= middle, component, component - middle)
    angles = (frequency * cell % NPSI) * (2.0 * math.pi / NPSI)
    return np.where(component <= middle, np.cos(angles), np.sin(angles)) / math.sqrt(NPSI)


def first_matrix():
    psi = psi_matrix()
    out = np.zeros((2, HALF, NPSI, NPSI, HIGH))
    for parity in range(2):
        for a in range(HIGH):
            sign = -1.0 if parity == 1 and a >= HALF else 1.0
            out[parity, a % HALF, :, :, a] = sign * psi
    return out.reshape(2 * HALF * NPSI, NPSI * HIGH)


def second_tables(groups):
    orders = NPHI // 2 // groups
    width = round_up(orders, LANES)
    f = np.arange(NPHI // 2)
    out = np.zeros((2, NPHI // 2, groups, width))
    for parity in range(2):
        k = np.arange(orders // 2)
        m = np.arange(groups)[:, None] * orders + 2 * k[None, :] + parity
        angles = (f[:, None, None] * m[None] % NPHI) * (2.0 * math.pi / NPHI)
        out[parity, :, :, 0:orders:2] = np.cos(angles)
        out[parity, :, :, 1:orders:2] = np.sin(angles)
    out = out / math.sqrt(NPHI)
    return out.reshape(2, NPHI // 2, groups * width), width


def dot(a, b, ca, cb):
    return lax.dot_general(a, b, (((ca,), (cb,)), ((), ())), preferred_element_type=F32)


def pack_kernel(groups, me_ref, *refs):
    sources, (out_ref, targets_ref), held, sems = refs[:6], refs[6:8], refs[8:14], refs[14]
    copies = [
        pltpu.make_async_copy(source, place, sems.at[number])
        for number, (source, place) in enumerate(zip(sources, held))
    ]
    for copy in copies:
        copy.start()
    owner_ref, signal_ref, weight_ref, cycle_ref, phi_ref, psi_ref = held
    copies[0].wait()
    for offset in range(targets_ref.shape[0]):
        targets_ref[offset] = me_ref[0] ^ offset
    blocks = owner_ref.shape[1]
    padded = out_ref.shape[2]
    owner = owner_ref[...]
    rows = round_up(groups, 8)
    hits = (owner == lax.broadcasted_iota(jnp.int32, (rows, blocks), 0)).astype(F32)
    before = (
        lax.broadcasted_iota(jnp.int32, (blocks, blocks), 0)
        < lax.broadcasted_iota(jnp.int32, (blocks, blocks), 1)
    ).astype(F32)
    earlier = dot(hits.astype(BF16), before.astype(BF16), 1, 0)
    within = jnp.sum(earlier * hits, axis=0, keepdims=True)
    position = owner * padded + within.astype(jnp.int32)
    spread = (
        (position == lax.broadcasted_iota(jnp.int32, (groups * padded, blocks), 0))
        .astype(F32)
        .astype(BF16)
    )
    for copy in copies[1:]:
        copy.wait()
    value = (signal_ref[...] * weight_ref[...]).astype(BF16)
    phi = phi_ref[...]
    high = (psi_ref[...] * HIGH + phi // LOW).astype(F32).astype(BF16)
    low = phi % LOW + 1
    low = jnp.where(cycle_ref[...] == 0, low, -low).astype(F32).astype(BF16)
    for number, plane in enumerate((value, high, low)):
        moved = dot(spread, plane, 1, 0).astype(BF16)
        for group in range(groups):
            out_ref[group, number] = moved[group * padded : (group + 1) * padded]


def bin_kernel(share, step, targets_ref, recv_ref, first_ref, second_ref, wigner_ref, out_ref, *rest):
    *held_refs, acc_ref, first_vmem, table_ref, first_sem, sem, held_sem = rest
    first_copy = pltpu.make_async_copy(first_ref, first_vmem, first_sem)
    first_copy.start()
    groups, _, padded, _ = recv_ref.shape
    width = out_ref.shape[-1]
    copy = pltpu.make_async_copy(second_ref, table_ref, sem)
    copy.start()
    held = []
    size = held_refs[0].shape[0]
    for offset, held_ref in enumerate(held_refs):
        source = wigner_ref.at[pl.ds(targets_ref[offset] * size, size), :]
        held.append(pltpu.make_async_copy(source, held_ref, held_sem.at[offset]))
        held[-1].start()
    acc_ref[...] = jnp.zeros_like(acc_ref)
    places = lax.broadcasted_iota(jnp.int32, (LOW, LANES), 0).astype(F32)
    places_hi = places.astype(BF16)
    places_lo = (places + 1.0).astype(BF16)
    zero = jnp.zeros((LOW, LANES), BF16)
    one = jnp.ones((LOW, LANES), BF16)

    def one_source(source, carry):
        for start in range(0, padded, step):
            value = recv_ref[source, 0, start : start + step, :]
            high = recv_ref[source, 1, start : start + step, :]
            low = recv_ref[source, 2, start : start + step, :]
            parts = [[], [], []]
            blank = jnp.zeros_like(value)
            value0 = jnp.where(low > 0, value, blank)
            value1 = jnp.where(low > 0, blank, value)
            low = jnp.abs(low)
            for row in range(step):
                same = places_hi == high[row : row + 1, :]
                parts[0].append(jnp.where(same, value0[row : row + 1, :], zero))
                parts[1].append(jnp.where(same, value1[row : row + 1, :], zero))
                parts[2].append(jnp.where(places_lo == low[row : row + 1, :], one, zero))
            left0 = jnp.concatenate(parts[0], axis=1)
            left1 = jnp.concatenate(parts[1], axis=1)
            right = jnp.concatenate(parts[2], axis=1)
            acc_ref[0] += dot(left0, right, 1, 1)
            acc_ref[1] += dot(left1, right, 1, 1)
        return carry

    lax.fori_loop(0, groups, one_source, 0)
    first_copy.wait()
    first = first_vmem[...]
    mixed = [dot(first, acc_ref[t].astype(BF16), 1, 0).astype(BF16) for t in range(CYCLE_DEV)]
    copy.wait()
    for parity in range(2):
        total = None
        for a0 in range(HALF):
            base = (parity * HALF + a0) * NPSI
            left = jnp.concatenate([part[base : base + NPSI] for part in mixed], axis=0)
            term = dot(left, table_ref[parity, a0 * LOW : (a0 + 1) * LOW, :], 1, 0)
            total = term if total is None else total + term
        total = total.astype(BF16)
        for group in range(groups):
            for beam in range(NPSI // share):
                for t in range(CYCLE_DEV):
                    base = t * NPSI + beam * share
                    out_ref[group, beam, parity, t] = total[
                        base : base + share, group * width : (group + 1) * width
                    ]
    for one in held:
        one.wait()


def coeff_kernel(groups, orders, recv_ref, out_ref):
    _, beams, _, cycles, share, width = recv_ref.shape
    thetas = groups * cycles
    depth = thetas * share
    row = lax.broadcasted_iota(jnp.int32, (depth, depth), 0)
    column = lax.broadcasted_iota(jnp.int32, (depth, depth), 1)
    swap = ((row % share) * thetas + row // share == column).astype(F32).astype(BF16)
    total = None
    for parity in range(2):
        parts = []
        for group in range(groups):
            for t in range(cycles):
                piece = recv_ref[group, 0, parity, t].astype(F32)
                for beam in range(1, beams):
                    piece = piece + recv_ref[group, beam, parity, t].astype(F32)
                parts.append(piece)
        stacked = jnp.concatenate(parts, axis=0).astype(BF16)
        turned = dot(stacked, swap, 0, 0).astype(BF16)
        row = lax.broadcasted_iota(jnp.int32, (2 * orders, width), 0)
        column = lax.broadcasted_iota(jnp.int32, (2 * orders, width), 1)
        place = (row // 4 * 2 + row % 2 == column) & (row // 2 % 2 == parity)
        term = dot(place.astype(F32).astype(BF16), turned, 1, 0)
        total = term if total is None else total + term
    out_ref[...] = total.astype(BF16)


def order_kernel(chunk, where_ref, coeff_ref, wigner_ref, out_ref):
    depth = coeff_ref.shape[1]
    step = pl.program_id(0)
    coeff = coeff_ref[...]
    wide = jnp.concatenate([coeff] * chunk, axis=1)
    row = lax.broadcasted_iota(jnp.int32, wide.shape, 0) // 2
    column = lax.broadcasted_iota(jnp.int32, wide.shape, 1) // depth
    wide = jnp.where(row == column, wide.astype(F32), 0.0).astype(BF16)
    out_ref[...] = dot(wide, wigner_ref[pl.ds(step * chunk * depth, chunk * depth), :], 1, 0).astype(out_ref.dtype)


def shards(signal, weight, cycle, phi, psi, owner, wigner):
    groups = lax.axis_size("blk")
    beams = lax.axis_size("beam")
    blocks = owner.shape[0]
    cap = max(2, 5 * blocks // (2 * groups))
    padded = round_up(cap, 8)
    share = NPSI // beams
    orders = wigner.shape[0]
    ells = wigner.shape[3]
    depth = share * groups * CYCLE_DEV

    def square(data):
        return pltpu.with_memory_space_constraint(data.reshape(blocks, BLOCK_ROWS), pltpu.HBM)

    whole = pl.BlockSpec(memory_space=pltpu.VMEM)
    scalars = pl.BlockSpec(memory_space=pltpu.SMEM)
    anywhere = pl.BlockSpec(memory_space=pl.ANY)
    me = lax.axis_index("beam").astype(jnp.int32)
    shape = (blocks, BLOCK_ROWS)
    sent, targets = pl.pallas_call(
        lambda *refs: pack_kernel(groups, *refs),
        out_shape=(
            jax.ShapeDtypeStruct((groups, 3, padded, BLOCK_ROWS), BF16),
            jax.ShapeDtypeStruct((beams,), jnp.int32),
        ),
        in_specs=[scalars] + [anywhere] * 6,
        out_specs=(whole, scalars),
        scratch_shapes=[pltpu.VMEM((1, blocks), jnp.int32)]
        + [pltpu.VMEM(shape, F32)] * 2
        + [pltpu.VMEM(shape, jnp.int32)] * 3
        + [pltpu.SemaphoreType.DMA((6,))],
        compiler_params=pltpu.CompilerParams(vmem_limit_bytes=6 << 20),
        name="pack",
    )(
        me.reshape(1),
        pltpu.with_memory_space_constraint(owner.reshape(1, blocks), pltpu.HBM),
        square(signal),
        square(weight),
        square(cycle),
        square(phi),
        square(psi),
    )
    got = lax.all_to_all(sent, "blk", split_axis=0, concat_axis=0, tiled=True)
    tables, width = second_tables(groups)
    flat = wigner.reshape(orders * depth, ells)
    spectra, *held = pl.pallas_call(
        lambda *refs: bin_kernel(share, 8, *refs),
        out_shape=(
            jax.ShapeDtypeStruct((groups, beams, 2, CYCLE_DEV, share, width), BF16),
        )
        + tuple(pltpu.VMEM((flat.shape[0] // beams, ells), BF16) for _ in range(beams)),
        in_specs=[scalars, whole, anywhere, anywhere, anywhere],
        out_specs=(whole,) * (1 + beams),
        scratch_shapes=[
            pltpu.VMEM((CYCLE_DEV, LOW, LOW), F32),
            pltpu.VMEM((LOW, LOW), BF16),
            pltpu.VMEM(tables.shape, BF16),
            pltpu.SemaphoreType.DMA,
            pltpu.SemaphoreType.DMA,
            pltpu.SemaphoreType.DMA((beams,)),
        ],
        compiler_params=pltpu.CompilerParams(vmem_limit_bytes=2 * tables.size + (4 << 20)),
        name="bin",
    )(
        targets,
        got,
        pltpu.with_memory_space_constraint(jnp.asarray(first_matrix(), BF16), pltpu.HBM),
        pltpu.with_memory_space_constraint(jnp.asarray(tables, BF16), pltpu.HBM),
        flat,
    )
    rows = 2 * CYCLE_DEV * share
    spectra = spectra.reshape(groups * beams, rows, width)
    parts = lax.all_to_all(spectra, ("blk", "beam"), split_axis=0, concat_axis=0, tiled=True)
    parts = parts.reshape(groups, beams, 2, CYCLE_DEV, share, width)
    coeff = pl.pallas_call(
        lambda *refs: coeff_kernel(groups, orders, *refs),
        out_shape=jax.ShapeDtypeStruct((2 * orders, depth), BF16),
        compiler_params=pltpu.CompilerParams(vmem_limit_bytes=6 << 20),
        name="coeff",
    )(parts)

    mine = orders // beams
    chunk = 8
    steps = mine // chunk

    def piece(offset, kind):
        return pl.pallas_call(
            lambda *refs: order_kernel(chunk, *refs),
            out_shape=jax.ShapeDtypeStruct((2 * mine, ells), kind),
            grid_spec=pltpu.PrefetchScalarGridSpec(
                num_scalar_prefetch=1,
                grid=(steps,),
                in_specs=[
                    pl.BlockSpec((2 * chunk, depth), lambda i, at: (at[offset] * steps + i, 0)),
                    pl.BlockSpec(memory_space=pltpu.VMEM),
                ],
                out_specs=pl.BlockSpec((2 * chunk, ells), lambda i, at: (i, 0)),
            ),
            compiler_params=pltpu.CompilerParams(vmem_limit_bytes=6 << 20),
            name="order",
        )(targets, coeff, pltpu.with_memory_space_constraint(held[offset], pltpu.VMEM))

    total = None
    for offset in range(beams - 1, -1, -1):
        part = piece(offset, BF16 if offset else F32)
        if offset:
            part = lax.ppermute(part, "beam", [(i, i ^ offset) for i in range(beams)])
        part = part.astype(F32)
        total = part if total is None else total + part
    return total.reshape(mine, 2, ells)


def solution(mesh):
    return jax.shard_map(
        shards,
        mesh=mesh,
        in_specs=(
            P(("blk", "beam")),
            P(("blk", "beam")),
            P(("blk", "beam")),
            P(("blk", "beam")),
            P(("blk", "beam")),
            P(("blk", "beam"), None),
            P("blk", "beam", None, None),
        ),
        out_specs=P(("blk", "beam"), None, None),
        check_vma=False,
    )
```

```python
import math

import jax
import jax.numpy as jnp
import numpy as np
from jax import lax
from jax.experimental import pallas as pl
from jax.experimental.pallas import tpu as pltpu
from jax.sharding import PartitionSpec as P


BLOCK_ROWS = 128
CYCLE_DEV = 2
NPSI = 32
NPHI = 2048
LOW = 256
HIGH = NPHI // LOW
HALF = HIGH // 2
LANES = 128
F32 = jnp.float32
BF16 = jnp.bfloat16


def round_up(value, step):
    return -(-value // step) * step


def psi_matrix():
    component = np.arange(NPSI)[:, None]
    cell = np.arange(NPSI)[None, :]
    middle = NPSI // 2
    frequency = np.where(component <= middle, component, component - middle)
    angles = (frequency * cell % NPSI) * (2.0 * math.pi / NPSI)
    return np.where(component <= middle, np.cos(angles), np.sin(angles)) / math.sqrt(NPSI)


def first_matrix():
    psi = psi_matrix()
    out = np.zeros((2, HALF, NPSI, NPSI, HIGH))
    for parity in range(2):
        for a in range(HIGH):
            sign = -1.0 if parity == 1 and a >= HALF else 1.0
            out[parity, a % HALF, :, :, a] = sign * psi
    return out.reshape(2 * HALF * NPSI, NPSI * HIGH)


def second_tables(groups):
    orders = NPHI // 2 // groups
    width = round_up(orders, LANES)
    f = np.arange(NPHI // 2)
    out = np.zeros((2, NPHI // 2, groups, width))
    for parity in range(2):
        k = np.arange(orders // 2)
        m = np.arange(groups)[:, None] * orders + 2 * k[None, :] + parity
        angles = (f[:, None, None] * m[None] % NPHI) * (2.0 * math.pi / NPHI)
        out[parity, :, :, 0:orders:2] = np.cos(angles)
        out[parity, :, :, 1:orders:2] = np.sin(angles)
    out = out / math.sqrt(NPHI)
    return out.reshape(2, NPHI // 2, groups * width), width


def dot(a, b, ca, cb):
    return lax.dot_general(a, b, (((ca,), (cb,)), ((), ())), preferred_element_type=F32)


def pack_kernel(groups, me_ref, *refs):
    sources, (out_ref, targets_ref), held, sems = refs[:6], refs[6:8], refs[8:14], refs[14]
    copies = [
        pltpu.make_async_copy(source, place, sems.at[number])
        for number, (source, place) in enumerate(zip(sources, held))
    ]
    for copy in copies:
        copy.start()
    owner_ref, signal_ref, weight_ref, cycle_ref, phi_ref, psi_ref = held
    copies[0].wait()
    for offset in range(targets_ref.shape[0]):
        targets_ref[offset] = me_ref[0] ^ offset
    blocks = owner_ref.shape[1]
    padded = out_ref.shape[2]
    owner = owner_ref[...]
    rows = round_up(groups, 8)
    hits = (owner == lax.broadcasted_iota(jnp.int32, (rows, blocks), 0)).astype(F32)
    before = (
        lax.broadcasted_iota(jnp.int32, (blocks, blocks), 0)
        < lax.broadcasted_iota(jnp.int32, (blocks, blocks), 1)
    ).astype(F32)
    earlier = dot(hits.astype(BF16), before.astype(BF16), 1, 0)
    within = jnp.sum(earlier * hits, axis=0, keepdims=True)
    position = owner * padded + within.astype(jnp.int32)
    spread = (
        (position == lax.broadcasted_iota(jnp.int32, (groups * padded, blocks), 0))
        .astype(F32)
        .astype(BF16)
    )
    for copy in copies[1:]:
        copy.wait()
    value = (signal_ref[...] * weight_ref[...]).astype(BF16)
    phi = phi_ref[...]
    high = (psi_ref[...] * HIGH + phi // LOW).astype(F32).astype(BF16)
    low = phi % LOW + 1
    low = jnp.where(cycle_ref[...] == 0, low, -low).astype(F32).astype(BF16)
    for number, plane in enumerate((value, high, low)):
        moved = dot(spread, plane, 1, 0).astype(BF16)
        for group in range(groups):
            out_ref[group, number] = moved[group * padded : (group + 1) * padded]


def network(count):
    size = 1
    while size < count:
        size *= 2
    pairs = []
    run = 1
    while run < size:
        gap = run
        while gap >= 1:
            for base in range(gap % run, size - gap, 2 * gap):
                for i in range(base, min(base + gap, size - gap)):
                    if i // (2 * run) == (i + gap) // (2 * run) and i + gap < count:
                        pairs.append((i, i + gap))
            gap //= 2
        run *= 2
    return pairs


def sort_tiles(tiles, first, last):
    for i, j in network(last - first):
        i, j = i + first, j + first
        (value0, high0, low0), (value1, high1, low1) = tiles[i], tiles[j]
        swap = low0 < low1
        tiles[i] = (jnp.where(swap, value1, value0), jnp.where(swap, high1, high0), jnp.maximum(low0, low1))
        tiles[j] = (jnp.where(swap, value0, value1), jnp.where(swap, high0, high1), jnp.minimum(low0, low1))


def bin_kernel(share, unit, targets_ref, recv_ref, first_ref, second_ref, wigner_ref, out_ref, *rest):
    *held_refs, sorted_ref, acc_ref, first_vmem, table_ref, first_sem, sem, held_sem = rest
    first_copy = pltpu.make_async_copy(first_ref, first_vmem, first_sem)
    first_copy.start()
    groups, _, padded, _ = recv_ref.shape
    width = out_ref.shape[-1]
    copy = pltpu.make_async_copy(second_ref, table_ref, sem)
    copy.start()
    held = []
    size = held_refs[0].shape[0]
    for offset, held_ref in enumerate(held_refs):
        source = wigner_ref.at[pl.ds(targets_ref[offset] * size, size), :]
        held.append(pltpu.make_async_copy(source, held_ref, held_sem.at[offset]))
        held[-1].start()
    acc_ref[...] = jnp.zeros_like(acc_ref)
    places = lax.broadcasted_iota(jnp.int32, (LOW, LANES), 0).astype(F32)
    places_hi = places.astype(BF16)
    places_lo = (places + 1.0).astype(BF16)
    zero = jnp.zeros((LOW, LANES), BF16)
    one = jnp.ones((LOW, LANES), BF16)

    tiles = [
        tuple(recv_ref[source, plane, start : start + 8, :].astype(F32) for plane in range(3))
        for source in range(groups)
        for start in range(0, padded, 8)
    ]
    count = len(tiles)
    sort_tiles(tiles, 0, count)
    start, stop = count // 5, count - count // 5
    for number in range(start, stop):
        tiles[number] = tuple(pltpu.roll(x, number * 29 % LANES, 1) for x in tiles[number])
    sort_tiles(tiles, start, stop)
    end0 = jnp.zeros((8, LANES), F32)
    for number in range(count):
        end0 = jnp.where(tiles[number][2] > 0, float(number + 1), end0)
    begin1 = jnp.full((8, LANES), float(count), F32)
    for number in range(count - 1, -1, -1):
        begin1 = jnp.where(tiles[number][2] < 0, float(number), begin1)
    for number in range(count):
        for plane in range(3):
            sorted_ref[plane, number] = tiles[number][plane].astype(BF16)

    def one_unit(t, number, carry):
        for step in range(unit):
            value, high, low = (sorted_ref[plane, number * unit + step] for plane in range(3))
            blank = jnp.zeros_like(value)
            value = jnp.where(low > 0, value, blank) if t == 0 else jnp.where(low > 0, blank, value)
            low = jnp.abs(low)
            left, right = [], []
            for row in range(8):
                left.append(jnp.where(places_hi == high[row : row + 1, :], value[row : row + 1, :], zero))
                right.append(jnp.where(places_lo == low[row : row + 1, :], one, zero))
            acc_ref[t] += dot(jnp.concatenate(left, axis=1), jnp.concatenate(right, axis=1), 1, 1)
        return carry

    end0 = lax.div(jnp.max(end0).astype(jnp.int32) + (unit - 1), unit)
    begin1 = lax.div(jnp.min(begin1).astype(jnp.int32), unit)
    lax.fori_loop(0, end0, lambda number, carry: one_unit(0, number, carry), 0)
    lax.fori_loop(begin1, count // unit, lambda number, carry: one_unit(1, number, carry), 0)
    first_copy.wait()
    first = first_vmem[...]
    mixed = [dot(first, acc_ref[t].astype(BF16), 1, 0).astype(BF16) for t in range(CYCLE_DEV)]
    copy.wait()
    for parity in range(2):
        total = None
        for a0 in range(HALF):
            base = (parity * HALF + a0) * NPSI
            left = jnp.concatenate([part[base : base + NPSI] for part in mixed], axis=0)
            term = dot(left, table_ref[parity, a0 * LOW : (a0 + 1) * LOW, :], 1, 0)
            total = term if total is None else total + term
        total = total.astype(BF16)
        for group in range(groups):
            for beam in range(NPSI // share):
                for t in range(CYCLE_DEV):
                    base = t * NPSI + beam * share
                    out_ref[group, beam, parity, t] = total[
                        base : base + share, group * width : (group + 1) * width
                    ]
    for one in held:
        one.wait()


def coeff_kernel(groups, orders, recv_ref, out_ref):
    _, beams, _, cycles, share, width = recv_ref.shape
    thetas = groups * cycles
    depth = thetas * share
    row = lax.broadcasted_iota(jnp.int32, (depth, depth), 0)
    column = lax.broadcasted_iota(jnp.int32, (depth, depth), 1)
    swap = ((row % share) * thetas + row // share == column).astype(F32).astype(BF16)
    total = None
    for parity in range(2):
        parts = []
        for group in range(groups):
            for t in range(cycles):
                piece = recv_ref[group, 0, parity, t].astype(F32)
                for beam in range(1, beams):
                    piece = piece + recv_ref[group, beam, parity, t].astype(F32)
                parts.append(piece)
        stacked = jnp.concatenate(parts, axis=0).astype(BF16)
        turned = dot(stacked, swap, 0, 0).astype(BF16)
        row = lax.broadcasted_iota(jnp.int32, (2 * orders, width), 0)
        column = lax.broadcasted_iota(jnp.int32, (2 * orders, width), 1)
        place = (row // 4 * 2 + row % 2 == column) & (row // 2 % 2 == parity)
        term = dot(place.astype(F32).astype(BF16), turned, 1, 0)
        total = term if total is None else total + term
    out_ref[...] = total.astype(BF16)


def order_kernel(chunk, offset, where_ref, coeff_ref, wigner_ref, out_ref):
    depth = coeff_ref.shape[1]
    rows = out_ref.shape[0]
    base = where_ref[offset] * rows
    shape = (2 * chunk, chunk * depth)
    own = lax.broadcasted_iota(jnp.int32, shape, 0) // 2 == lax.broadcasted_iota(jnp.int32, shape, 1) // depth
    for number in range(rows // (2 * chunk)):
        start = pl.multiple_of(base + number * 2 * chunk, 2 * chunk)
        coeff = coeff_ref[pl.ds(start, 2 * chunk), :].astype(F32)
        wide = jnp.where(own, jnp.concatenate([coeff] * chunk, axis=1), 0.0).astype(BF16)
        part = dot(wide, wigner_ref[number * chunk * depth : (number + 1) * chunk * depth, :], 1, 0)
        out_ref[number * 2 * chunk : (number + 1) * 2 * chunk, :] = part.astype(out_ref.dtype)


def shards(signal, weight, cycle, phi, psi, owner, wigner):
    groups = lax.axis_size("blk")
    beams = lax.axis_size("beam")
    blocks = owner.shape[0]
    cap = max(2, 5 * blocks // (2 * groups))
    padded = round_up(cap, 8)
    share = NPSI // beams
    orders = wigner.shape[0]
    ells = wigner.shape[3]
    depth = share * groups * CYCLE_DEV

    def square(data):
        return pltpu.with_memory_space_constraint(data.reshape(blocks, BLOCK_ROWS), pltpu.HBM)

    whole = pl.BlockSpec(memory_space=pltpu.VMEM)
    scalars = pl.BlockSpec(memory_space=pltpu.SMEM)
    anywhere = pl.BlockSpec(memory_space=pl.ANY)
    me = lax.axis_index("beam").astype(jnp.int32)
    shape = (blocks, BLOCK_ROWS)
    sent, targets = pl.pallas_call(
        lambda *refs: pack_kernel(groups, *refs),
        out_shape=(
            jax.ShapeDtypeStruct((groups, 3, padded, BLOCK_ROWS), BF16),
            jax.ShapeDtypeStruct((beams,), jnp.int32),
        ),
        in_specs=[scalars] + [anywhere] * 6,
        out_specs=(whole, scalars),
        scratch_shapes=[pltpu.VMEM((1, blocks), jnp.int32)]
        + [pltpu.VMEM(shape, F32)] * 2
        + [pltpu.VMEM(shape, jnp.int32)] * 3
        + [pltpu.SemaphoreType.DMA((6,))],
        compiler_params=pltpu.CompilerParams(vmem_limit_bytes=6 << 20),
        name="pack",
    )(
        me.reshape(1),
        pltpu.with_memory_space_constraint(owner.reshape(1, blocks), pltpu.HBM),
        square(signal),
        square(weight),
        square(cycle),
        square(phi),
        square(psi),
    )
    got = lax.all_to_all(sent, "blk", split_axis=0, concat_axis=0, tiled=True)
    tables, width = second_tables(groups)
    tiles = groups * padded // 8
    unit = next(size for size in (5, 4, 2, 1) if tiles % size == 0)
    flat = wigner.reshape(orders * depth, ells)
    spectra, *held = pl.pallas_call(
        lambda *refs: bin_kernel(share, unit, *refs),
        out_shape=(
            jax.ShapeDtypeStruct((groups, beams, 2, CYCLE_DEV, share, width), BF16),
        )
        + tuple(pltpu.VMEM((flat.shape[0] // beams, ells), BF16) for _ in range(beams)),
        in_specs=[scalars, whole, anywhere, anywhere, anywhere],
        out_specs=(whole,) * (1 + beams),
        scratch_shapes=[
            pltpu.VMEM((3, tiles, 8, LANES), BF16),
            pltpu.VMEM((CYCLE_DEV, LOW, LOW), F32),
            pltpu.VMEM((LOW, LOW), BF16),
            pltpu.VMEM(tables.shape, BF16),
            pltpu.SemaphoreType.DMA,
            pltpu.SemaphoreType.DMA,
            pltpu.SemaphoreType.DMA((beams,)),
        ],
        compiler_params=pltpu.CompilerParams(vmem_limit_bytes=2 * tables.size + (4 << 20)),
        name="bin",
    )(
        targets,
        got,
        pltpu.with_memory_space_constraint(jnp.asarray(first_matrix(), BF16), pltpu.HBM),
        pltpu.with_memory_space_constraint(jnp.asarray(tables, BF16), pltpu.HBM),
        flat,
    )
    rows = 2 * CYCLE_DEV * share
    spectra = spectra.reshape(groups * beams, rows, width)
    parts = lax.all_to_all(spectra, ("blk", "beam"), split_axis=0, concat_axis=0, tiled=True)
    parts = parts.reshape(groups, beams, 2, CYCLE_DEV, share, width)
    coeff = pl.pallas_call(
        lambda *refs: coeff_kernel(groups, orders, *refs),
        out_shape=jax.ShapeDtypeStruct((2 * orders, depth), BF16),
        compiler_params=pltpu.CompilerParams(vmem_limit_bytes=6 << 20),
        name="coeff",
    )(parts)

    mine = orders // beams
    chunk = 8

    def piece(offset, kind):
        return pl.pallas_call(
            lambda *refs: order_kernel(chunk, offset, *refs),
            out_shape=jax.ShapeDtypeStruct((2 * mine, ells), kind),
            in_specs=[scalars, whole, whole],
            out_specs=whole,
            compiler_params=pltpu.CompilerParams(vmem_limit_bytes=6 << 20),
            name="order",
        )(targets, coeff, pltpu.with_memory_space_constraint(held[offset], pltpu.VMEM))

    total = None
    for offset in range(beams - 1, -1, -1):
        part = piece(offset, BF16 if offset else F32)
        if offset:
            part = lax.ppermute(part, "beam", [(i, i ^ offset) for i in range(beams)])
        part = part.astype(F32)
        total = part if total is None else total + part
    return total.reshape(mine, 2, ells)


def solution(mesh):
    return jax.shard_map(
        shards,
        mesh=mesh,
        in_specs=(
            P(("blk", "beam")),
            P(("blk", "beam")),
            P(("blk", "beam")),
            P(("blk", "beam")),
            P(("blk", "beam")),
            P(("blk", "beam"), None),
            P("blk", "beam", None, None),
        ),
        out_specs=P(("blk", "beam"), None, None),
        check_vma=False,
    )
```

```python
import math

import jax
import jax.numpy as jnp
import numpy as np
from jax import lax
from jax.experimental import pallas as pl
from jax.experimental.pallas import tpu as pltpu
from jax.sharding import PartitionSpec as P


BLOCK_ROWS = 128
CYCLE_DEV = 2
NPSI = 32
NPHI = 2048
LOW = 256
HIGH = NPHI // LOW
HALF = HIGH // 2
LANES = 128
F32 = jnp.float32
BF16 = jnp.bfloat16


def round_up(value, step):
    return -(-value // step) * step


def psi_matrix():
    component = np.arange(NPSI)[:, None]
    cell = np.arange(NPSI)[None, :]
    middle = NPSI // 2
    frequency = np.where(component <= middle, component, component - middle)
    angles = (frequency * cell % NPSI) * (2.0 * math.pi / NPSI)
    return np.where(component <= middle, np.cos(angles), np.sin(angles)) / math.sqrt(NPSI)


def first_matrix():
    psi = psi_matrix()
    out = np.zeros((2, HALF, NPSI, NPSI, HIGH))
    for parity in range(2):
        for a in range(HIGH):
            sign = -1.0 if parity == 1 and a >= HALF else 1.0
            out[parity, a % HALF, :, :, a] = sign * psi
    return out.reshape(2 * HALF * NPSI, NPSI * HIGH)


def second_tables(groups):
    orders = NPHI // 2 // groups
    width = round_up(orders, LANES)
    f = np.arange(NPHI // 2)
    out = np.zeros((2, NPHI // 2, groups, width))
    for parity in range(2):
        k = np.arange(orders // 2)
        m = np.arange(groups)[:, None] * orders + 2 * k[None, :] + parity
        angles = (f[:, None, None] * m[None] % NPHI) * (2.0 * math.pi / NPHI)
        out[parity, :, :, 0:orders:2] = np.cos(angles)
        out[parity, :, :, 1:orders:2] = np.sin(angles)
    out = out / math.sqrt(NPHI)
    return out.reshape(2, NPHI // 2, groups * width), width


def dot(a, b, ca, cb):
    return lax.dot_general(a, b, (((ca,), (cb,)), ((), ())), preferred_element_type=F32)


def pack_kernel(groups, me_ref, *refs):
    sources, (out_ref, targets_ref), held, sems = refs[:6], refs[6:8], refs[8:14], refs[14]
    copies = [
        pltpu.make_async_copy(source, place, sems.at[number])
        for number, (source, place) in enumerate(zip(sources, held))
    ]
    for copy in copies:
        copy.start()
    owner_ref, signal_ref, weight_ref, cycle_ref, phi_ref, psi_ref = held
    copies[0].wait()
    for offset in range(targets_ref.shape[0]):
        targets_ref[offset] = me_ref[0] ^ offset
    blocks = owner_ref.shape[1]
    padded = out_ref.shape[2]
    owner = owner_ref[...]
    rows = round_up(groups, 8)
    hits = (owner == lax.broadcasted_iota(jnp.int32, (rows, blocks), 0)).astype(F32)
    before = (
        lax.broadcasted_iota(jnp.int32, (blocks, blocks), 0)
        < lax.broadcasted_iota(jnp.int32, (blocks, blocks), 1)
    ).astype(F32)
    earlier = dot(hits.astype(BF16), before.astype(BF16), 1, 0)
    within = jnp.sum(earlier * hits, axis=0, keepdims=True)
    position = owner * padded + within.astype(jnp.int32)
    spread = (
        (position == lax.broadcasted_iota(jnp.int32, (groups * padded, blocks), 0))
        .astype(F32)
        .astype(BF16)
    )
    for copy in copies[1:]:
        copy.wait()
    value = (signal_ref[...] * weight_ref[...]).astype(BF16)
    phi = phi_ref[...]
    high = (psi_ref[...] * HIGH + phi // LOW).astype(F32).astype(BF16)
    low = phi % LOW + 1
    low = jnp.where(cycle_ref[...] == 0, low, -low).astype(F32).astype(BF16)
    for number, plane in enumerate((value, high, low)):
        moved = dot(spread, plane, 1, 0).astype(BF16)
        for group in range(groups):
            out_ref[group, number] = moved[group * padded : (group + 1) * padded]


def network(count):
    size = 1
    while size < count:
        size *= 2
    pairs = []
    run = 1
    while run < size:
        gap = run
        while gap >= 1:
            for base in range(gap % run, size - gap, 2 * gap):
                for i in range(base, min(base + gap, size - gap)):
                    if i // (2 * run) == (i + gap) // (2 * run) and i + gap < count:
                        pairs.append((i, i + gap))
            gap //= 2
        run *= 2
    return pairs


def sort_tiles(tiles, first, last):
    for i, j in network(last - first):
        i, j = i + first, j + first
        (value0, high0, low0), (value1, high1, low1) = tiles[i], tiles[j]
        swap = low0 < low1
        tiles[i] = (jnp.where(swap, value1, value0), jnp.where(swap, high1, high0), jnp.maximum(low0, low1))
        tiles[j] = (jnp.where(swap, value0, value1), jnp.where(swap, high0, high1), jnp.minimum(low0, low1))


def bin_kernel(share, unit, targets_ref, recv_ref, first_ref, second_ref, wigner_ref, out_ref, *rest):
    *held_refs, sorted_ref, acc_ref, first_vmem, table_ref, first_sem, sem, held_sem = rest
    first_copy = pltpu.make_async_copy(first_ref, first_vmem, first_sem)
    first_copy.start()
    groups, _, padded, _ = recv_ref.shape
    width = out_ref.shape[-1]
    copy = pltpu.make_async_copy(second_ref, table_ref, sem)
    copy.start()
    held = []
    size = held_refs[0].shape[0]
    for number, held_ref in enumerate(held_refs):
        source = wigner_ref.at[pl.ds(targets_ref[number + 1] * size, size), :]
        held.append(pltpu.make_async_copy(source, held_ref, held_sem.at[number]))
        held[-1].start()
    acc_ref[...] = jnp.zeros_like(acc_ref)
    places = lax.broadcasted_iota(jnp.int32, (LOW, LANES), 0).astype(F32)
    places_hi = places.astype(BF16)
    places_lo = (places + 1.0).astype(BF16)
    zero = jnp.zeros((LOW, LANES), BF16)
    one = jnp.ones((LOW, LANES), BF16)

    tiles = [
        tuple(recv_ref[source, plane, start : start + 8, :].astype(F32) for plane in range(3))
        for source in range(groups)
        for start in range(0, padded, 8)
    ]
    count = len(tiles)
    sort_tiles(tiles, 0, count)
    start, stop = count // 5, count - count // 5
    for number in range(start, stop):
        tiles[number] = tuple(pltpu.roll(x, number * 29 % LANES, 1) for x in tiles[number])
    sort_tiles(tiles, start, stop)
    end0 = jnp.zeros((8, LANES), F32)
    for number in range(count):
        end0 = jnp.where(tiles[number][2] > 0, float(number + 1), end0)
    begin1 = jnp.full((8, LANES), float(count), F32)
    for number in range(count - 1, -1, -1):
        begin1 = jnp.where(tiles[number][2] < 0, float(number), begin1)
    for number in range(count):
        for plane in range(3):
            sorted_ref[plane, number] = tiles[number][plane].astype(BF16)

    def one_unit(t, number, carry):
        for step in range(unit):
            value, high, low = (sorted_ref[plane, number * unit + step] for plane in range(3))
            blank = jnp.zeros_like(value)
            value = jnp.where(low > 0, value, blank) if t == 0 else jnp.where(low > 0, blank, value)
            low = jnp.abs(low)
            left, right = [], []
            for row in range(8):
                left.append(jnp.where(places_hi == high[row : row + 1, :], value[row : row + 1, :], zero))
                right.append(jnp.where(places_lo == low[row : row + 1, :], one, zero))
            acc_ref[t] += dot(jnp.concatenate(left, axis=1), jnp.concatenate(right, axis=1), 1, 1)
        return carry

    end0 = lax.div(jnp.max(end0).astype(jnp.int32) + (unit - 1), unit)
    begin1 = lax.div(jnp.min(begin1).astype(jnp.int32), unit)
    lax.fori_loop(0, end0, lambda number, carry: one_unit(0, number, carry), 0)
    lax.fori_loop(begin1, count // unit, lambda number, carry: one_unit(1, number, carry), 0)
    first_copy.wait()
    first = first_vmem[...]
    mixed = [dot(first, acc_ref[t].astype(BF16), 1, 0).astype(BF16) for t in range(CYCLE_DEV)]
    copy.wait()
    for parity in range(2):
        total = None
        for a0 in range(HALF):
            base = (parity * HALF + a0) * NPSI
            left = jnp.concatenate([part[base : base + NPSI] for part in mixed], axis=0)
            term = dot(left, table_ref[parity, a0 * LOW : (a0 + 1) * LOW, :], 1, 0)
            total = term if total is None else total + term
        total = total.astype(BF16)
        for group in range(groups):
            for beam in range(NPSI // share):
                for t in range(CYCLE_DEV):
                    base = t * NPSI + beam * share
                    out_ref[group, beam, parity, t] = total[
                        base : base + share, group * width : (group + 1) * width
                    ]
    for one in held:
        one.wait()


def coeff_kernel(groups, orders, recv_ref, out_ref):
    _, beams, _, cycles, share, width = recv_ref.shape
    thetas = groups * cycles
    depth = thetas * share
    row = lax.broadcasted_iota(jnp.int32, (depth, depth), 0)
    column = lax.broadcasted_iota(jnp.int32, (depth, depth), 1)
    swap = ((row % share) * thetas + row // share == column).astype(F32).astype(BF16)
    total = None
    for parity in range(2):
        parts = []
        for group in range(groups):
            for t in range(cycles):
                piece = recv_ref[group, 0, parity, t].astype(F32)
                for beam in range(1, beams):
                    piece = piece + recv_ref[group, beam, parity, t].astype(F32)
                parts.append(piece)
        stacked = jnp.concatenate(parts, axis=0).astype(BF16)
        turned = dot(stacked, swap, 0, 0).astype(BF16)
        row = lax.broadcasted_iota(jnp.int32, (2 * orders, width), 0)
        column = lax.broadcasted_iota(jnp.int32, (2 * orders, width), 1)
        place = (row // 4 * 2 + row % 2 == column) & (row // 2 % 2 == parity)
        term = dot(place.astype(F32).astype(BF16), turned, 1, 0)
        total = term if total is None else total + term
    out_ref[...] = total.astype(BF16)


def order_kernel(chunk, offset, fetch, tables, where_ref, coeff_ref, *refs):
    depth = coeff_ref.shape[1]
    size = chunk * depth
    wigner_refs, refs = refs[:tables], refs[tables:]
    copies = []
    if fetch:
        source_ref, out_ref, *held_refs, sem = refs
        for number, held_ref in zip(fetch, held_refs):
            first = where_ref[0] * (out_ref.shape[0] * depth // 2) + number * size
            source = source_ref.at[pl.ds(first, size), :]
            copies.append(pltpu.make_async_copy(source, held_ref, sem.at[len(copies)]))
            copies[-1].start()
    else:
        (out_ref,) = refs
    rows = out_ref.shape[0]
    base = where_ref[offset] * rows
    shape = (2 * chunk, size)
    own = lax.broadcasted_iota(jnp.int32, shape, 0) // 2 == lax.broadcasted_iota(jnp.int32, shape, 1) // depth
    number = 0
    for wigner_ref in wigner_refs:
        for first in range(0, wigner_ref.shape[0], size):
            start = pl.multiple_of(base + number * 2 * chunk, 2 * chunk)
            coeff = coeff_ref[pl.ds(start, 2 * chunk), :].astype(F32)
            wide = jnp.where(own, jnp.concatenate([coeff] * chunk, axis=1), 0.0).astype(BF16)
            part = dot(wide, wigner_ref[first : first + size, :], 1, 0)
            out_ref[number * 2 * chunk : (number + 1) * 2 * chunk, :] = part.astype(out_ref.dtype)
            number += 1
    for copy in copies:
        copy.wait()


def shards(signal, weight, cycle, phi, psi, owner, wigner):
    groups = lax.axis_size("blk")
    beams = lax.axis_size("beam")
    blocks = owner.shape[0]
    cap = max(2, 5 * blocks // (2 * groups))
    padded = round_up(cap, 8)
    share = NPSI // beams
    orders = wigner.shape[0]
    ells = wigner.shape[3]
    depth = share * groups * CYCLE_DEV

    def square(data):
        return pltpu.with_memory_space_constraint(data.reshape(blocks, BLOCK_ROWS), pltpu.HBM)

    whole = pl.BlockSpec(memory_space=pltpu.VMEM)
    scalars = pl.BlockSpec(memory_space=pltpu.SMEM)
    anywhere = pl.BlockSpec(memory_space=pl.ANY)
    me = lax.axis_index("beam").astype(jnp.int32)
    shape = (blocks, BLOCK_ROWS)
    sent, targets = pl.pallas_call(
        lambda *refs: pack_kernel(groups, *refs),
        out_shape=(
            jax.ShapeDtypeStruct((groups, 3, padded, BLOCK_ROWS), BF16),
            jax.ShapeDtypeStruct((beams,), jnp.int32),
        ),
        in_specs=[scalars] + [anywhere] * 6,
        out_specs=(whole, scalars),
        scratch_shapes=[pltpu.VMEM((1, blocks), jnp.int32)]
        + [pltpu.VMEM(shape, F32)] * 2
        + [pltpu.VMEM(shape, jnp.int32)] * 3
        + [pltpu.SemaphoreType.DMA((6,))],
        compiler_params=pltpu.CompilerParams(vmem_limit_bytes=6 << 20),
        name="pack",
    )(
        me.reshape(1),
        pltpu.with_memory_space_constraint(owner.reshape(1, blocks), pltpu.HBM),
        square(signal),
        square(weight),
        square(cycle),
        square(phi),
        square(psi),
    )
    got = lax.all_to_all(sent, "blk", split_axis=0, concat_axis=0, tiled=True)
    tables, width = second_tables(groups)
    tiles = groups * padded // 8
    unit = next(size for size in (5, 4, 2, 1) if tiles % size == 0)
    flat = wigner.reshape(orders * depth, ells)
    spectra, *held = pl.pallas_call(
        lambda *refs: bin_kernel(share, unit, *refs),
        out_shape=(
            jax.ShapeDtypeStruct((groups, beams, 2, CYCLE_DEV, share, width), BF16),
        )
        + tuple(pltpu.VMEM((flat.shape[0] // beams, ells), BF16) for _ in range(beams - 1)),
        in_specs=[scalars, whole, anywhere, anywhere, anywhere],
        out_specs=(whole,) * beams,
        scratch_shapes=[
            pltpu.VMEM((3, tiles, 8, LANES), BF16),
            pltpu.VMEM((CYCLE_DEV, LOW, LOW), F32),
            pltpu.VMEM((LOW, LOW), BF16),
            pltpu.VMEM(tables.shape, BF16),
            pltpu.SemaphoreType.DMA,
            pltpu.SemaphoreType.DMA,
            pltpu.SemaphoreType.DMA((beams - 1,)),
        ],
        compiler_params=pltpu.CompilerParams(vmem_limit_bytes=2 * tables.size + (4 << 20)),
        name="bin",
    )(
        targets,
        got,
        pltpu.with_memory_space_constraint(jnp.asarray(first_matrix(), BF16), pltpu.HBM),
        pltpu.with_memory_space_constraint(jnp.asarray(tables, BF16), pltpu.HBM),
        flat,
    )
    rows = 2 * CYCLE_DEV * share
    spectra = spectra.reshape(groups * beams, rows, width)
    parts = lax.all_to_all(spectra, ("blk", "beam"), split_axis=0, concat_axis=0, tiled=True)
    parts = parts.reshape(groups, beams, 2, CYCLE_DEV, share, width)
    coeff = pl.pallas_call(
        lambda *refs: coeff_kernel(groups, orders, *refs),
        out_shape=jax.ShapeDtypeStruct((2 * orders, depth), BF16),
        compiler_params=pltpu.CompilerParams(vmem_limit_bytes=6 << 20),
        name="coeff",
    )(parts)

    mine = orders // beams
    chunk = 8
    parts = mine // chunk
    last = {}

    def piece(offset, fetch, kind):
        tables = [held[offset - 1]] if offset else [last[number] for number in range(parts)]
        tables = [pltpu.with_memory_space_constraint(table, pltpu.VMEM) for table in tables]
        source = [pltpu.with_memory_space_constraint(flat, pltpu.HBM)] if fetch else []
        part, *fetched = pl.pallas_call(
            lambda *refs: order_kernel(chunk, offset, fetch, len(tables), *refs),
            out_shape=(jax.ShapeDtypeStruct((2 * mine, ells), kind),)
            + tuple(pltpu.VMEM((chunk * depth, ells), BF16) for _ in fetch),
            in_specs=[scalars] + [whole] * (1 + len(tables)) + [anywhere] * len(source),
            out_specs=(whole,) * (1 + len(fetch)),
            scratch_shapes=[pltpu.SemaphoreType.DMA((len(fetch),))] if fetch else [],
            compiler_params=pltpu.CompilerParams(vmem_limit_bytes=6 << 20),
            name="order",
        )(targets, coeff, *tables, *source)
        last.update(zip(fetch, fetched))
        return part

    def send(part, distance):
        return lax.ppermute(part, "beam", [(i, i ^ distance) for i in range(beams)])

    sequence = [offset for chip in range(beams // 2 - 1, -1, -1) for offset in (2 * chip + 1, 2 * chip)]
    shares_of = {offset: [] for offset in sequence}
    for number in range(parts):
        shares_of[sequence[number % (beams - 1)]].append(number)
    terms = []
    near = None
    for offset in sequence:
        fetch = sorted(shares_of[offset])
        part = piece(offset, fetch, BF16 if offset % 2 else F32)
        if offset % 2:
            near = send(part, 1)
        else:
            part = part + near.astype(F32)
            terms.append(send(part.astype(BF16), offset).astype(F32) if offset else part)
    total = terms[-1]
    for term in terms[:-1]:
        total = total + term
    return total.reshape(mine, 2, ells)


def solution(mesh):
    return jax.shard_map(
        shards,
        mesh=mesh,
        in_specs=(
            P(("blk", "beam")),
            P(("blk", "beam")),
            P(("blk", "beam")),
            P(("blk", "beam")),
            P(("blk", "beam")),
            P(("blk", "beam"), None),
            P("blk", "beam", None, None),
        ),
        out_specs=P(("blk", "beam"), None, None),
        check_vma=False,
    )
```

```python
import math

import jax
import jax.numpy as jnp
import numpy as np
from jax import lax
from jax.experimental import pallas as pl
from jax.experimental.pallas import tpu as pltpu
from jax.sharding import PartitionSpec as P


BLOCK_ROWS = 128
CYCLE_DEV = 2
NPSI = 32
NPHI = 2048
LOW = 256
HIGH = NPHI // LOW
HALF = HIGH // 2
LANES = 128
F32 = jnp.float32
BF16 = jnp.bfloat16


def round_up(value, step):
    return -(-value // step) * step


def psi_matrix():
    component = np.arange(NPSI)[:, None]
    cell = np.arange(NPSI)[None, :]
    middle = NPSI // 2
    frequency = np.where(component <= middle, component, component - middle)
    angles = (frequency * cell % NPSI) * (2.0 * math.pi / NPSI)
    return np.where(component <= middle, np.cos(angles), np.sin(angles)) / math.sqrt(NPSI)


def first_matrix():
    psi = psi_matrix()
    out = np.zeros((2, HALF, NPSI, NPSI, HIGH))
    for parity in range(2):
        for a in range(HIGH):
            sign = -1.0 if parity == 1 and a >= HALF else 1.0
            out[parity, a % HALF, :, :, a] = sign * psi
    return out.reshape(2 * HALF * NPSI, NPSI * HIGH)


def second_tables(groups):
    orders = NPHI // 2 // groups
    width = round_up(orders, LANES)
    f = np.arange(NPHI // 2)
    out = np.zeros((2, NPHI // 2, groups, width))
    for parity in range(2):
        k = np.arange(orders // 2)
        m = np.arange(groups)[:, None] * orders + 2 * k[None, :] + parity
        angles = (f[:, None, None] * m[None] % NPHI) * (2.0 * math.pi / NPHI)
        out[parity, :, :, 0:orders:2] = np.cos(angles)
        out[parity, :, :, 1:orders:2] = np.sin(angles)
    out = out / math.sqrt(NPHI)
    return out.reshape(2, NPHI // 2, groups * width), width


def dot(a, b, ca, cb):
    return lax.dot_general(a, b, (((ca,), (cb,)), ((), ())), preferred_element_type=F32)


def pack_kernel(groups, me_ref, *refs):
    sources, (out_ref, targets_ref), held, sems = refs[:6], refs[6:8], refs[8:14], refs[14]
    copies = [
        pltpu.make_async_copy(source, place, sems.at[number])
        for number, (source, place) in enumerate(zip(sources, held))
    ]
    for copy in copies:
        copy.start()
    owner_ref, signal_ref, weight_ref, cycle_ref, phi_ref, psi_ref = held
    copies[0].wait()
    for offset in range(targets_ref.shape[0]):
        targets_ref[offset] = me_ref[0] ^ offset
    blocks = owner_ref.shape[1]
    padded = out_ref.shape[2]
    owner = owner_ref[...]
    rows = round_up(groups, 8)
    hits = (owner == lax.broadcasted_iota(jnp.int32, (rows, blocks), 0)).astype(F32)
    before = (
        lax.broadcasted_iota(jnp.int32, (blocks, blocks), 0)
        < lax.broadcasted_iota(jnp.int32, (blocks, blocks), 1)
    ).astype(F32)
    earlier = dot(hits.astype(BF16), before.astype(BF16), 1, 0)
    within = jnp.sum(earlier * hits, axis=0, keepdims=True)
    position = owner * padded + within.astype(jnp.int32)
    spread = (
        (position == lax.broadcasted_iota(jnp.int32, (groups * padded, blocks), 0))
        .astype(F32)
        .astype(BF16)
    )
    for copy in copies[1:]:
        copy.wait()
    value = (signal_ref[...] * weight_ref[...]).astype(BF16)
    phi = phi_ref[...]
    high = (psi_ref[...] * HIGH + phi // LOW).astype(F32).astype(BF16)
    low = phi % LOW + 1
    low = jnp.where(cycle_ref[...] == 0, low, -low).astype(F32).astype(BF16)
    for number, plane in enumerate((value, high, low)):
        moved = dot(spread, plane, 1, 0).astype(BF16)
        for group in range(groups):
            out_ref[group, number] = moved[group * padded : (group + 1) * padded]


def network(count):
    size = 1
    while size < count:
        size *= 2
    pairs = []
    run = 1
    while run < size:
        gap = run
        while gap >= 1:
            for base in range(gap % run, size - gap, 2 * gap):
                for i in range(base, min(base + gap, size - gap)):
                    if i // (2 * run) == (i + gap) // (2 * run) and i + gap < count:
                        pairs.append((i, i + gap))
            gap //= 2
        run *= 2
    return pairs


def sort_tiles(tiles, first, last):
    for i, j in network(last - first):
        i, j = i + first, j + first
        (value0, high0, low0), (value1, high1, low1) = tiles[i], tiles[j]
        swap = low0 < low1
        tiles[i] = (jnp.where(swap, value1, value0), jnp.where(swap, high1, high0), jnp.maximum(low0, low1))
        tiles[j] = (jnp.where(swap, value0, value1), jnp.where(swap, high0, high1), jnp.minimum(low0, low1))


def bin_kernel(share, unit, targets_ref, recv_ref, first_ref, second_ref, wigner_ref, out_ref, *rest):
    *held_refs, sorted_ref, acc_ref, first_vmem, table_ref, first_sem, sem, held_sem = rest
    first_copy = pltpu.make_async_copy(first_ref, first_vmem, first_sem)
    first_copy.start()
    groups, _, padded, _ = recv_ref.shape
    width = out_ref.shape[-1]
    copy = pltpu.make_async_copy(second_ref, table_ref, sem)
    copy.start()
    held = []
    size = held_refs[0].shape[0]
    for number, held_ref in enumerate(held_refs):
        source = wigner_ref.at[pl.ds(targets_ref[number] * size, size), :]
        held.append(pltpu.make_async_copy(source, held_ref, held_sem.at[number]))
        held[-1].start()
    acc_ref[...] = jnp.zeros_like(acc_ref)
    places = lax.broadcasted_iota(jnp.int32, (LOW, LANES), 0).astype(F32)
    places_hi = places.astype(BF16)
    places_lo = (places + 1.0).astype(BF16)
    zero = jnp.zeros((LOW, LANES), BF16)
    one = jnp.ones((LOW, LANES), BF16)

    tiles = [
        tuple(recv_ref[source, plane, start : start + 8, :].astype(F32) for plane in range(3))
        for source in range(groups)
        for start in range(0, padded, 8)
    ]
    count = len(tiles)
    sort_tiles(tiles, 0, count)
    start, stop = count // 5, count - count // 5
    for number in range(start, stop):
        tiles[number] = tuple(pltpu.roll(x, number * 29 % LANES, 1) for x in tiles[number])
    sort_tiles(tiles, start, stop)
    end0 = jnp.zeros((8, LANES), F32)
    for number in range(count):
        end0 = jnp.where(tiles[number][2] > 0, float(number + 1), end0)
    begin1 = jnp.full((8, LANES), float(count), F32)
    for number in range(count - 1, -1, -1):
        begin1 = jnp.where(tiles[number][2] < 0, float(number), begin1)
    for number in range(count):
        for plane in range(3):
            sorted_ref[plane, number] = tiles[number][plane].astype(BF16)

    def one_unit(t, number, carry):
        for step in range(unit):
            value, high, low = (sorted_ref[plane, number * unit + step] for plane in range(3))
            blank = jnp.zeros_like(value)
            value = jnp.where(low > 0, value, blank) if t == 0 else jnp.where(low > 0, blank, value)
            low = jnp.abs(low)
            left, right = [], []
            for row in range(8):
                left.append(jnp.where(places_hi == high[row : row + 1, :], value[row : row + 1, :], zero))
                right.append(jnp.where(places_lo == low[row : row + 1, :], one, zero))
            acc_ref[t] += dot(jnp.concatenate(left, axis=1), jnp.concatenate(right, axis=1), 1, 1)
        return carry

    end0 = lax.div(jnp.max(end0).astype(jnp.int32) + (unit - 1), unit)
    begin1 = lax.div(jnp.min(begin1).astype(jnp.int32), unit)
    lax.fori_loop(0, end0, lambda number, carry: one_unit(0, number, carry), 0)
    lax.fori_loop(begin1, count // unit, lambda number, carry: one_unit(1, number, carry), 0)
    first_copy.wait()
    first = first_vmem[...]
    mixed = [dot(first, acc_ref[t].astype(BF16), 1, 0).astype(BF16) for t in range(CYCLE_DEV)]
    copy.wait()
    for parity in range(2):
        total = None
        for a0 in range(HALF):
            base = (parity * HALF + a0) * NPSI
            left = jnp.concatenate([part[base : base + NPSI] for part in mixed], axis=0)
            term = dot(left, table_ref[parity, a0 * LOW : (a0 + 1) * LOW, :], 1, 0)
            total = term if total is None else total + term
        total = total.astype(BF16)
        for group in range(groups):
            for beam in range(NPSI // share):
                for t in range(CYCLE_DEV):
                    base = t * NPSI + beam * share
                    out_ref[group, beam, parity, t] = total[
                        base : base + share, group * width : (group + 1) * width
                    ]
    for one in held:
        one.wait()


def coeff_kernel(groups, orders, recv_ref, out_ref):
    _, beams, _, cycles, share, width = recv_ref.shape
    thetas = groups * cycles
    depth = thetas * share
    row = lax.broadcasted_iota(jnp.int32, (depth, depth), 0)
    column = lax.broadcasted_iota(jnp.int32, (depth, depth), 1)
    swap = ((row % share) * thetas + row // share == column).astype(F32).astype(BF16)
    total = None
    for parity in range(2):
        parts = []
        for group in range(groups):
            for t in range(cycles):
                piece = recv_ref[group, 0, parity, t].astype(F32)
                for beam in range(1, beams):
                    piece = piece + recv_ref[group, beam, parity, t].astype(F32)
                parts.append(piece)
        stacked = jnp.concatenate(parts, axis=0).astype(BF16)
        turned = dot(stacked, swap, 0, 0).astype(BF16)
        row = lax.broadcasted_iota(jnp.int32, (2 * orders, width), 0)
        column = lax.broadcasted_iota(jnp.int32, (2 * orders, width), 1)
        place = (row // 4 * 2 + row % 2 == column) & (row // 2 % 2 == parity)
        term = dot(place.astype(F32).astype(BF16), turned, 1, 0)
        total = term if total is None else total + term
    out_ref[...] = total.astype(BF16)


def order_kernel(chunk, offset, where_ref, coeff_ref, wigner_ref, out_ref):
    depth = coeff_ref.shape[1]
    size = chunk * depth
    rows = out_ref.shape[0]
    base = where_ref[offset] * rows
    shape = (2 * chunk, size)
    own = lax.broadcasted_iota(jnp.int32, shape, 0) // 2 == lax.broadcasted_iota(jnp.int32, shape, 1) // depth
    for number in range(rows // (2 * chunk)):
        start = pl.multiple_of(base + number * 2 * chunk, 2 * chunk)
        coeff = coeff_ref[pl.ds(start, 2 * chunk), :].astype(F32)
        wide = jnp.where(own, jnp.concatenate([coeff] * chunk, axis=1), 0.0).astype(BF16)
        part = dot(wide, wigner_ref[number * size : (number + 1) * size, :], 1, 0)
        out_ref[number * 2 * chunk : (number + 1) * 2 * chunk, :] = part.astype(out_ref.dtype)


def shards(signal, weight, cycle, phi, psi, owner, wigner):
    groups = lax.axis_size("blk")
    beams = lax.axis_size("beam")
    blocks = owner.shape[0]
    cap = max(2, 5 * blocks // (2 * groups))
    padded = round_up(cap, 8)
    share = NPSI // beams
    orders = wigner.shape[0]
    ells = wigner.shape[3]
    depth = share * groups * CYCLE_DEV

    def square(data):
        return pltpu.with_memory_space_constraint(data.reshape(blocks, BLOCK_ROWS), pltpu.HBM)

    whole = pl.BlockSpec(memory_space=pltpu.VMEM)
    scalars = pl.BlockSpec(memory_space=pltpu.SMEM)
    anywhere = pl.BlockSpec(memory_space=pl.ANY)
    me = lax.axis_index("beam").astype(jnp.int32)
    shape = (blocks, BLOCK_ROWS)
    sent, targets = pl.pallas_call(
        lambda *refs: pack_kernel(groups, *refs),
        out_shape=(
            jax.ShapeDtypeStruct((groups, 3, padded, BLOCK_ROWS), BF16),
            jax.ShapeDtypeStruct((beams,), jnp.int32),
        ),
        in_specs=[scalars] + [anywhere] * 6,
        out_specs=(whole, scalars),
        scratch_shapes=[pltpu.VMEM((1, blocks), jnp.int32)]
        + [pltpu.VMEM(shape, F32)] * 2
        + [pltpu.VMEM(shape, jnp.int32)] * 3
        + [pltpu.SemaphoreType.DMA((6,))],
        compiler_params=pltpu.CompilerParams(vmem_limit_bytes=6 << 20),
        cost_estimate=pl.CostEstimate(flops=10**11, transcendentals=0, bytes_accessed=10**8),
        name="pack",
    )(
        me.reshape(1),
        pltpu.with_memory_space_constraint(owner.reshape(1, blocks), pltpu.HBM),
        square(signal),
        square(weight),
        square(cycle),
        square(phi),
        square(psi),
    )
    got = lax.all_to_all(sent, "blk", split_axis=0, concat_axis=0, tiled=True)
    tables, width = second_tables(groups)
    tiles = groups * padded // 8
    unit = next(size for size in (5, 4, 2, 1) if tiles % size == 0)
    flat = wigner.reshape(orders * depth, ells)
    spectra, *held = pl.pallas_call(
        lambda *refs: bin_kernel(share, unit, *refs),
        out_shape=(
            jax.ShapeDtypeStruct((groups, beams, 2, CYCLE_DEV, share, width), BF16),
        )
        + tuple(pltpu.VMEM((flat.shape[0] // beams, ells), BF16) for _ in range(beams)),
        in_specs=[scalars, whole, anywhere, anywhere, anywhere],
        out_specs=(whole,) * (1 + beams),
        scratch_shapes=[
            pltpu.VMEM((3, tiles, 8, LANES), BF16),
            pltpu.VMEM((CYCLE_DEV, LOW, LOW), F32),
            pltpu.VMEM((LOW, LOW), BF16),
            pltpu.VMEM(tables.shape, BF16),
            pltpu.SemaphoreType.DMA,
            pltpu.SemaphoreType.DMA,
            pltpu.SemaphoreType.DMA((beams,)),
        ],
        compiler_params=pltpu.CompilerParams(vmem_limit_bytes=2 * tables.size + (4 << 20)),
        name="bin",
    )(
        targets,
        got,
        pltpu.with_memory_space_constraint(jnp.asarray(first_matrix(), BF16), pltpu.HBM),
        jnp.asarray(tables, BF16),
        pltpu.with_memory_space_constraint(flat, pltpu.HBM),
    )
    rows = 2 * CYCLE_DEV * share
    spectra = spectra.reshape(groups * beams, rows, width)
    parts = lax.all_to_all(spectra, ("blk", "beam"), split_axis=0, concat_axis=0, tiled=True)
    parts = parts.reshape(groups, beams, 2, CYCLE_DEV, share, width)
    coeff = pl.pallas_call(
        lambda *refs: coeff_kernel(groups, orders, *refs),
        out_shape=jax.ShapeDtypeStruct((2 * orders, depth), BF16),
        compiler_params=pltpu.CompilerParams(vmem_limit_bytes=6 << 20),
        name="coeff",
    )(parts)

    mine = orders // beams
    chunk = 8

    def piece(offset, kind):
        return pl.pallas_call(
            lambda *refs: order_kernel(chunk, offset, *refs),
            out_shape=jax.ShapeDtypeStruct((2 * mine, ells), kind),
            in_specs=[scalars, whole, whole],
            out_specs=whole,
            compiler_params=pltpu.CompilerParams(vmem_limit_bytes=6 << 20),
            name="order",
        )(targets, coeff, pltpu.with_memory_space_constraint(held[offset], pltpu.VMEM))

    def send(part, distance):
        return lax.ppermute(part, "beam", [(i, i ^ distance) for i in range(beams)])

    sequence = [offset for chip in range(beams // 2 - 1, -1, -1) for offset in (2 * chip + 1, 2 * chip)]
    terms = []
    near = None
    for offset in sequence:
        part = piece(offset, BF16 if offset % 2 else F32)
        if offset % 2:
            near = send(part, 1)
        else:
            part = part + near.astype(F32)
            terms.append(send(part.astype(BF16), offset).astype(F32) if offset else part)
    total = terms[-1]
    for term in terms[:-1]:
        total = total + term
    return total.reshape(mine, 2, ells)


def solution(mesh):
    return jax.shard_map(
        shards,
        mesh=mesh,
        in_specs=(
            P(("blk", "beam")),
            P(("blk", "beam")),
            P(("blk", "beam")),
            P(("blk", "beam")),
            P(("blk", "beam")),
            P(("blk", "beam"), None),
            P("blk", "beam", None, None),
        ),
        out_specs=P(("blk", "beam"), None, None),
        check_vma=False,
    )
```

```python
import math

import jax
import jax.numpy as jnp
import numpy as np
from jax import lax
from jax.experimental import pallas as pl
from jax.experimental.pallas import tpu as pltpu
from jax.sharding import PartitionSpec as P


BLOCK_ROWS = 128
CYCLE_DEV = 2
NPSI = 32
NPHI = 2048
LOW = 256
HIGH = NPHI // LOW
HALF = HIGH // 2
LANES = 128
F32 = jnp.float32
BF16 = jnp.bfloat16


def round_up(value, step):
    return -(-value // step) * step


def psi_matrix():
    component = np.arange(NPSI)[:, None]
    cell = np.arange(NPSI)[None, :]
    middle = NPSI // 2
    frequency = np.where(component <= middle, component, component - middle)
    angles = (frequency * cell % NPSI) * (2.0 * math.pi / NPSI)
    return np.where(component <= middle, np.cos(angles), np.sin(angles)) / math.sqrt(NPSI)


def first_matrix():
    psi = psi_matrix()
    out = np.zeros((2, HALF, NPSI, NPSI, HIGH))
    for parity in range(2):
        for a in range(HIGH):
            sign = -1.0 if parity == 1 and a >= HALF else 1.0
            out[parity, a % HALF, :, :, a] = sign * psi
    return out.reshape(2 * HALF * NPSI, NPSI * HIGH)


def second_tables(groups):
    orders = NPHI // 2 // groups
    width = round_up(orders, LANES)
    f = np.arange(NPHI // 2)
    out = np.zeros((2, NPHI // 2, groups, width))
    for parity in range(2):
        k = np.arange(orders // 2)
        m = np.arange(groups)[:, None] * orders + 2 * k[None, :] + parity
        angles = (f[:, None, None] * m[None] % NPHI) * (2.0 * math.pi / NPHI)
        out[parity, :, :, 0:orders:2] = np.cos(angles)
        out[parity, :, :, 1:orders:2] = np.sin(angles)
    out = out / math.sqrt(NPHI)
    return out.reshape(2, NPHI // 2, groups * width), width


def dot(a, b, ca, cb):
    return lax.dot_general(a, b, (((ca,), (cb,)), ((), ())), preferred_element_type=F32)


def pack_kernel(groups, me_ref, *refs):
    sources, (out_ref, targets_ref), held, sems = refs[:6], refs[6:8], refs[8:14], refs[14]
    copies = [
        pltpu.make_async_copy(source, place, sems.at[number])
        for number, (source, place) in enumerate(zip(sources, held))
    ]
    for copy in copies:
        copy.start()
    owner_ref, signal_ref, weight_ref, cycle_ref, phi_ref, psi_ref = held
    copies[0].wait()
    for offset in range(targets_ref.shape[0]):
        targets_ref[offset] = me_ref[0] ^ offset
    blocks = owner_ref.shape[1]
    padded = out_ref.shape[2]
    owner = owner_ref[...]
    rows = round_up(groups, 8)
    hits = (owner == lax.broadcasted_iota(jnp.int32, (rows, blocks), 0)).astype(F32)
    before = (
        lax.broadcasted_iota(jnp.int32, (blocks, blocks), 0)
        < lax.broadcasted_iota(jnp.int32, (blocks, blocks), 1)
    ).astype(F32)
    earlier = dot(hits.astype(BF16), before.astype(BF16), 1, 0)
    within = jnp.sum(earlier * hits, axis=0, keepdims=True)
    position = owner * padded + within.astype(jnp.int32)
    spread = (
        (position == lax.broadcasted_iota(jnp.int32, (groups * padded, blocks), 0))
        .astype(F32)
        .astype(BF16)
    )
    for copy in copies[1:]:
        copy.wait()
    value = (signal_ref[...] * weight_ref[...]).astype(BF16)
    phi = phi_ref[...]
    high = (psi_ref[...] * HIGH + phi // LOW).astype(F32).astype(BF16)
    low = phi % LOW + 1
    low = jnp.where(cycle_ref[...] == 0, low, -low).astype(F32).astype(BF16)
    for number, plane in enumerate((value, high, low)):
        moved = dot(spread, plane, 1, 0).astype(BF16)
        for group in range(groups):
            out_ref[group, number] = moved[group * padded : (group + 1) * padded]


def network(count):
    size = 1
    while size < count:
        size *= 2
    pairs = []
    run = 1
    while run < size:
        gap = run
        while gap >= 1:
            for base in range(gap % run, size - gap, 2 * gap):
                for i in range(base, min(base + gap, size - gap)):
                    if i // (2 * run) == (i + gap) // (2 * run) and i + gap < count:
                        pairs.append((i, i + gap))
            gap //= 2
        run *= 2
    return pairs


def sort_tiles(tiles, first, last):
    for i, j in network(last - first):
        i, j = i + first, j + first
        (value0, code0), (value1, code1) = tiles[i], tiles[j]
        swap = code0 < code1
        tiles[i] = (jnp.where(swap, value1, value0), jnp.maximum(code0, code1))
        tiles[j] = (jnp.where(swap, value0, value1), jnp.minimum(code0, code1))


def bin_kernel(share, unit, targets_ref, recv_ref, first_ref, second_ref, wigner_ref, out_ref, *rest):
    *held_refs, sorted_ref, acc_ref, first_vmem, table_ref, first_sem, sem, held_sem = rest
    first_copy = pltpu.make_async_copy(first_ref, first_vmem, first_sem)
    first_copy.start()
    groups, _, padded, _ = recv_ref.shape
    width = out_ref.shape[-1]
    copy = pltpu.make_async_copy(second_ref, table_ref, sem)
    copy.start()
    held = []
    size = wigner_ref.shape[0] // len(held_refs)
    for number, held_ref in enumerate(held_refs):
        source = wigner_ref.at[pl.ds(targets_ref[number] * size, held_ref.shape[0]), :]
        held.append(pltpu.make_async_copy(source, held_ref, held_sem.at[number]))
        held[-1].start()
    acc_ref[...] = jnp.zeros_like(acc_ref)
    places = lax.broadcasted_iota(jnp.int32, (LOW, LANES), 0).astype(F32)
    places_hi = places.astype(BF16)
    places_lo = (places + 1.0).astype(BF16)
    zero = jnp.zeros((LOW, LANES), BF16)
    one = jnp.ones((LOW, LANES), BF16)

    tiles = []
    for source in range(groups):
        for start in range(0, padded, 8):
            value, high, low = (recv_ref[source, plane, start : start + 8, :].astype(F32) for plane in range(3))
            tiles.append((value, low + jnp.where(low > 0, high, -high) * float(LOW)))
    count = len(tiles)
    sort_tiles(tiles, 0, count)
    start, stop = count // 5, count - count // 5
    for number in range(start, stop):
        tiles[number] = tuple(pltpu.roll(x, number * 29 % LANES, 1) for x in tiles[number])
    sort_tiles(tiles, start, stop)
    end0 = jnp.zeros((8, LANES), F32)
    for number in range(count):
        end0 = jnp.where(tiles[number][1] > 0, float(number + 1), end0)
    begin1 = jnp.full((8, LANES), float(count), F32)
    for number in range(count - 1, -1, -1):
        begin1 = jnp.where(tiles[number][1] < 0, float(number), begin1)
    for number in range(count):
        value, code = tiles[number]
        place = jnp.abs(code)
        high = jnp.floor((place - 1.0) * (1.0 / LOW))
        low = place - high * float(LOW)
        sorted_ref[0, number] = jnp.where(code > 0, value, 0.0).astype(BF16)
        sorted_ref[1, number] = jnp.where(code > 0, 0.0, value).astype(BF16)
        sorted_ref[2, number] = high.astype(BF16)
        sorted_ref[3, number] = low.astype(BF16)

    def one_unit(t, number, carry):
        for step in range(unit):
            value, high, low = (sorted_ref[plane, number * unit + step] for plane in (t, 2, 3))
            left, right = [], []
            for row in range(8):
                left.append(jnp.where(places_hi == high[row : row + 1, :], value[row : row + 1, :], zero))
                right.append(jnp.where(places_lo == low[row : row + 1, :], one, zero))
            acc_ref[t] += dot(jnp.concatenate(left, axis=1), jnp.concatenate(right, axis=1), 1, 1)
        return carry

    end0 = lax.div(jnp.max(end0).astype(jnp.int32) + (unit - 1), unit)
    begin1 = lax.div(jnp.min(begin1).astype(jnp.int32), unit)
    lax.fori_loop(0, end0, lambda number, carry: one_unit(0, number, carry), 0)
    lax.fori_loop(begin1, count // unit, lambda number, carry: one_unit(1, number, carry), 0)
    first_copy.wait()
    first = first_vmem[...]
    mixed = [dot(first, acc_ref[t].astype(BF16), 1, 0).astype(BF16) for t in range(CYCLE_DEV)]
    copy.wait()
    for parity in range(2):
        total = None
        for a0 in range(HALF):
            base = (parity * HALF + a0) * NPSI
            left = jnp.concatenate([part[base : base + NPSI] for part in mixed], axis=0)
            term = dot(left, table_ref[parity, a0 * LOW : (a0 + 1) * LOW, :], 1, 0)
            total = term if total is None else total + term
        total = total.astype(BF16)
        for group in range(groups):
            for beam in range(NPSI // share):
                for t in range(CYCLE_DEV):
                    base = t * NPSI + beam * share
                    out_ref[group, beam, parity, t] = total[
                        base : base + share, group * width : (group + 1) * width
                    ]
    for one in held:
        one.wait()


def coeff_kernel(groups, orders, recv_ref, out_ref):
    _, beams, _, cycles, share, width = recv_ref.shape
    thetas = groups * cycles
    depth = thetas * share
    row = lax.broadcasted_iota(jnp.int32, (depth, depth), 0)
    column = lax.broadcasted_iota(jnp.int32, (depth, depth), 1)
    swap = ((row % share) * thetas + row // share == column).astype(F32).astype(BF16)
    total = None
    for parity in range(2):
        parts = []
        for group in range(groups):
            for t in range(cycles):
                piece = recv_ref[group, 0, parity, t].astype(F32)
                for beam in range(1, beams):
                    piece = piece + recv_ref[group, beam, parity, t].astype(F32)
                parts.append(piece)
        stacked = jnp.concatenate(parts, axis=0).astype(BF16)
        turned = dot(stacked, swap, 0, 0).astype(BF16)
        row = lax.broadcasted_iota(jnp.int32, (2 * orders, width), 0)
        column = lax.broadcasted_iota(jnp.int32, (2 * orders, width), 1)
        place = (row // 4 * 2 + row % 2 == column) & (row // 2 % 2 == parity)
        term = dot(place.astype(F32).astype(BF16), turned, 1, 0)
        total = term if total is None else total + term
    out_ref[...] = total.astype(BF16)


def order_kernel(chunk, offset, late, where_ref, coeff_ref, wigner_ref, *refs):
    depth = coeff_ref.shape[1]
    size = chunk * depth
    copy = None
    if late:
        source_ref, out_ref, late_ref, sem = refs
        rows = out_ref.shape[0]
        first = where_ref[offset] * (rows // 2 * depth) + wigner_ref.shape[0]
        copy = pltpu.make_async_copy(source_ref.at[pl.ds(first, late * size), :], late_ref, sem)
        copy.start()
    else:
        (out_ref,) = refs
        rows = out_ref.shape[0]
    base = where_ref[offset] * rows
    shape = (2 * chunk, size)
    own = lax.broadcasted_iota(jnp.int32, shape, 0) // 2 == lax.broadcasted_iota(jnp.int32, shape, 1) // depth
    early = wigner_ref.shape[0] // size
    for number in range(early + late):
        if number == early:
            copy.wait()
        table, at = (wigner_ref, number) if number < early else (late_ref, number - early)
        start = pl.multiple_of(base + number * 2 * chunk, 2 * chunk)
        coeff = coeff_ref[pl.ds(start, 2 * chunk), :].astype(F32)
        wide = jnp.where(own, jnp.concatenate([coeff] * chunk, axis=1), 0.0).astype(BF16)
        part = dot(wide, table[at * size : (at + 1) * size, :], 1, 0)
        out_ref[number * 2 * chunk : (number + 1) * 2 * chunk, :] = part.astype(out_ref.dtype)


def sum_kernel(*refs):
    *terms, out_ref = refs
    total = terms[0][...].astype(F32)
    for term in terms[1:]:
        total = total + term[...].astype(F32)
    out_ref[...] = total.reshape(out_ref.shape)


def shards(signal, weight, cycle, phi, psi, owner, wigner):
    groups = lax.axis_size("blk")
    beams = lax.axis_size("beam")
    blocks = owner.shape[0]
    cap = max(2, 5 * blocks // (2 * groups))
    padded = round_up(cap, 8)
    share = NPSI // beams
    orders = wigner.shape[0]
    ells = wigner.shape[3]
    depth = share * groups * CYCLE_DEV

    def square(data):
        return pltpu.with_memory_space_constraint(data.reshape(blocks, BLOCK_ROWS), pltpu.HBM)

    whole = pl.BlockSpec(memory_space=pltpu.VMEM)
    scalars = pl.BlockSpec(memory_space=pltpu.SMEM)
    anywhere = pl.BlockSpec(memory_space=pl.ANY)
    me = lax.axis_index("beam").astype(jnp.int32)
    shape = (blocks, BLOCK_ROWS)
    sent, targets = pl.pallas_call(
        lambda *refs: pack_kernel(groups, *refs),
        out_shape=(
            jax.ShapeDtypeStruct((groups, 3, padded, BLOCK_ROWS), BF16),
            jax.ShapeDtypeStruct((beams,), jnp.int32),
        ),
        in_specs=[scalars] + [anywhere] * 6,
        out_specs=(whole, scalars),
        scratch_shapes=[pltpu.VMEM((1, blocks), jnp.int32)]
        + [pltpu.VMEM(shape, F32)] * 2
        + [pltpu.VMEM(shape, jnp.int32)] * 3
        + [pltpu.SemaphoreType.DMA((6,))],
        compiler_params=pltpu.CompilerParams(vmem_limit_bytes=6 << 20),
        cost_estimate=pl.CostEstimate(flops=10**11, transcendentals=0, bytes_accessed=10**8),
        name="pack",
    )(
        me.reshape(1),
        pltpu.with_memory_space_constraint(owner.reshape(1, blocks), pltpu.HBM),
        square(signal),
        square(weight),
        square(cycle),
        square(phi),
        square(psi),
    )
    got = lax.all_to_all(sent, "blk", split_axis=0, concat_axis=0, tiled=True)
    tables, width = second_tables(groups)
    tiles = groups * padded // 8
    unit = next(size for size in (5, 4, 2, 1) if tiles % size == 0)
    flat = wigner.reshape(orders * depth, ells)
    mine = orders // beams
    chunk = 8
    steps = mine // chunk
    early = (steps + 1) // 2
    spectra, *held = pl.pallas_call(
        lambda *refs: bin_kernel(share, unit, *refs),
        out_shape=(
            jax.ShapeDtypeStruct((groups, beams, 2, CYCLE_DEV, share, width), BF16),
        )
        + tuple(pltpu.VMEM((count * chunk * depth, ells), BF16) for count in [early] + [steps] * (beams - 1)),
        in_specs=[scalars, whole, anywhere, anywhere, anywhere],
        out_specs=(whole,) * (1 + beams),
        scratch_shapes=[
            pltpu.VMEM((4, tiles, 8, LANES), BF16),
            pltpu.VMEM((CYCLE_DEV, LOW, LOW), F32),
            pltpu.VMEM((LOW, LOW), BF16),
            pltpu.VMEM(tables.shape, BF16),
            pltpu.SemaphoreType.DMA,
            pltpu.SemaphoreType.DMA,
            pltpu.SemaphoreType.DMA((beams,)),
        ],
        compiler_params=pltpu.CompilerParams(vmem_limit_bytes=2 * tables.size + (4 << 20)),
        name="bin",
    )(
        targets,
        got,
        pltpu.with_memory_space_constraint(jnp.asarray(first_matrix(), BF16), pltpu.HBM),
        jnp.asarray(tables, BF16),
        pltpu.with_memory_space_constraint(flat, pltpu.HBM),
    )
    rows = 2 * CYCLE_DEV * share
    spectra = spectra.reshape(groups * beams, rows, width)
    parts = lax.all_to_all(spectra, ("blk", "beam"), split_axis=0, concat_axis=0, tiled=True)
    parts = parts.reshape(groups, beams, 2, CYCLE_DEV, share, width)
    coeff = pl.pallas_call(
        lambda *refs: coeff_kernel(groups, orders, *refs),
        out_shape=jax.ShapeDtypeStruct((2 * orders, depth), BF16),
        compiler_params=pltpu.CompilerParams(vmem_limit_bytes=6 << 20),
        name="coeff",
    )(parts)

    def piece(offset, kind):
        late = 0 if offset else steps - early
        table = pltpu.with_memory_space_constraint(held[offset], pltpu.VMEM)
        source = [pltpu.with_memory_space_constraint(flat, pltpu.HBM)] if late else []
        scratch = [pltpu.VMEM((late * chunk * depth, ells), BF16), pltpu.SemaphoreType.DMA] if late else []
        return pl.pallas_call(
            lambda *refs: order_kernel(chunk, offset, late, *refs),
            out_shape=jax.ShapeDtypeStruct((2 * mine, ells), kind),
            in_specs=[scalars, whole, whole] + [anywhere] * len(source),
            out_specs=whole,
            scratch_shapes=scratch,
            compiler_params=pltpu.CompilerParams(vmem_limit_bytes=6 << 20),
            name="order",
        )(targets, coeff, table, *source)

    def send(part, distance):
        return lax.ppermute(part, "beam", [(i, i ^ distance) for i in range(beams)])

    sequence = [offset for chip in range(beams // 2 - 1, -1, -1) for offset in (2 * chip + 1, 2 * chip)]
    terms = []
    near = None
    for offset in sequence:
        part = piece(offset, BF16 if offset % 2 else F32)
        if offset % 2:
            near = send(part, 1)
        elif offset:
            terms.append(send((part + near.astype(F32)).astype(BF16), offset))
        else:
            terms = [part, near] + terms
    return pl.pallas_call(
        sum_kernel,
        out_shape=jax.ShapeDtypeStruct((mine, 2, ells), F32),
        compiler_params=pltpu.CompilerParams(vmem_limit_bytes=6 << 20),
        name="sum",
    )(*terms)


def solution(mesh):
    return jax.shard_map(
        shards,
        mesh=mesh,
        in_specs=(
            P(("blk", "beam")),
            P(("blk", "beam")),
            P(("blk", "beam")),
            P(("blk", "beam")),
            P(("blk", "beam")),
            P(("blk", "beam"), None),
            P("blk", "beam", None, None),
        ),
        out_specs=P(("blk", "beam"), None, None),
        check_vma=False,
    )
```

```python
import math

import jax
import jax.numpy as jnp
import numpy as np
from jax import lax
from jax.experimental import pallas as pl
from jax.experimental.pallas import tpu as pltpu
from jax.sharding import PartitionSpec as P


BLOCK_ROWS = 128
CYCLE_DEV = 2
NPSI = 32
NPHI = 2048
LOW = 256
HIGH = NPHI // LOW
HALF = HIGH // 2
LANES = 128
F32 = jnp.float32
BF16 = jnp.bfloat16


def round_up(value, step):
    return -(-value // step) * step


def psi_matrix():
    component = np.arange(NPSI)[:, None]
    cell = np.arange(NPSI)[None, :]
    middle = NPSI // 2
    frequency = np.where(component <= middle, component, component - middle)
    angles = (frequency * cell % NPSI) * (2.0 * math.pi / NPSI)
    return np.where(component <= middle, np.cos(angles), np.sin(angles)) / math.sqrt(NPSI)


def first_matrix():
    psi = psi_matrix()
    out = np.zeros((2, HALF, NPSI, NPSI, HIGH))
    for parity in range(2):
        for a in range(HIGH):
            sign = -1.0 if parity == 1 and a >= HALF else 1.0
            out[parity, a % HALF, :, :, a] = sign * psi
    return out.reshape(2 * HALF * NPSI, NPSI * HIGH)


def second_tables(groups):
    orders = NPHI // 2 // groups
    width = round_up(orders, LANES)
    f = np.arange(NPHI // 2)
    out = np.zeros((2, NPHI // 2, groups, width))
    for parity in range(2):
        k = np.arange(orders // 2)
        m = np.arange(groups)[:, None] * orders + 2 * k[None, :] + parity
        angles = (f[:, None, None] * m[None] % NPHI) * (2.0 * math.pi / NPHI)
        out[parity, :, :, 0:orders:2] = np.cos(angles)
        out[parity, :, :, 1:orders:2] = np.sin(angles)
    out = out / math.sqrt(NPHI)
    return out.reshape(2, NPHI // 2, groups * width), width


def dot(a, b, ca, cb):
    return lax.dot_general(a, b, (((ca,), (cb,)), ((), ())), preferred_element_type=F32)


def pack_kernel(groups, me_ref, *refs):
    sources, (out_ref, targets_ref), held, sems = refs[:6], refs[6:8], refs[8:14], refs[14]
    copies = [
        pltpu.make_async_copy(source, place, sems.at[number])
        for number, (source, place) in enumerate(zip(sources, held))
    ]
    for copy in copies:
        copy.start()
    owner_ref, signal_ref, weight_ref, cycle_ref, phi_ref, psi_ref = held
    copies[0].wait()
    for offset in range(targets_ref.shape[0]):
        targets_ref[offset] = me_ref[0] ^ offset
    blocks = owner_ref.shape[1]
    padded = out_ref.shape[2]
    owner = owner_ref[...]
    rows = round_up(groups, 8)
    hits = (owner == lax.broadcasted_iota(jnp.int32, (rows, blocks), 0)).astype(F32)
    before = (
        lax.broadcasted_iota(jnp.int32, (blocks, blocks), 0)
        < lax.broadcasted_iota(jnp.int32, (blocks, blocks), 1)
    ).astype(F32)
    earlier = dot(hits.astype(BF16), before.astype(BF16), 1, 0)
    within = jnp.sum(earlier * hits, axis=0, keepdims=True)
    position = owner * padded + within.astype(jnp.int32)
    spread = (
        (position == lax.broadcasted_iota(jnp.int32, (groups * padded, blocks), 0))
        .astype(F32)
        .astype(BF16)
    )
    for copy in copies[1:]:
        copy.wait()
    value = (signal_ref[...] * weight_ref[...]).astype(BF16)
    phi = phi_ref[...]
    high = (psi_ref[...] * HIGH + phi // LOW).astype(F32).astype(BF16)
    low = phi % LOW + 1
    low = jnp.where(cycle_ref[...] == 0, low, -low).astype(F32).astype(BF16)
    for number, plane in enumerate((value, high, low)):
        moved = dot(spread, plane, 1, 0).astype(BF16)
        for group in range(groups):
            out_ref[group, number] = moved[group * padded : (group + 1) * padded]


def network(count):
    size = 1
    while size < count:
        size *= 2
    pairs = []
    run = 1
    while run < size:
        gap = run
        while gap >= 1:
            for base in range(gap % run, size - gap, 2 * gap):
                for i in range(base, min(base + gap, size - gap)):
                    if i // (2 * run) == (i + gap) // (2 * run) and i + gap < count:
                        pairs.append((i, i + gap))
            gap //= 2
        run *= 2
    return pairs


def sort_tiles(tiles, first, last):
    for i, j in network(last - first):
        i, j = i + first, j + first
        (value0, code0), (value1, code1) = tiles[i], tiles[j]
        swap = code0 < code1
        tiles[i] = (jnp.where(swap, value1, value0), jnp.maximum(code0, code1))
        tiles[j] = (jnp.where(swap, value0, value1), jnp.minimum(code0, code1))


def bin_kernel(share, unit, targets_ref, recv_ref, first_ref, second_ref, wigner_ref, out_ref, *rest):
    *held_refs, sorted_ref, acc_ref, first_vmem, table_ref, first_sem, sem, held_sem = rest
    first_copy = pltpu.make_async_copy(first_ref, first_vmem, first_sem)
    first_copy.start()
    groups, _, padded, _ = recv_ref.shape
    width = out_ref.shape[-1]
    copy = pltpu.make_async_copy(second_ref, table_ref, sem)
    copy.start()
    held = []
    size = wigner_ref.shape[0] // len(held_refs)
    for number, held_ref in enumerate(held_refs):
        source = wigner_ref.at[pl.ds(targets_ref[number] * size, held_ref.shape[0]), :]
        held.append(pltpu.make_async_copy(source, held_ref, held_sem.at[number]))
        held[-1].start()
    acc_ref[...] = jnp.zeros_like(acc_ref)
    places = lax.broadcasted_iota(jnp.int32, (LOW, LANES), 0).astype(F32)
    places_hi = places.astype(BF16)
    places_lo = (places + 1.0).astype(BF16)
    zero = jnp.zeros((LOW, LANES), BF16)
    one = jnp.ones((LOW, LANES), BF16)

    tiles = []
    for source in range(groups):
        for start in range(0, padded, 8):
            value, high, low = (recv_ref[source, plane, start : start + 8, :].astype(F32) for plane in range(3))
            tiles.append((value, low + jnp.where(low > 0, high, -high) * float(LOW)))
    count = len(tiles)
    sort_tiles(tiles, 0, count)
    start, stop = count // 5, count - count // 5
    for number in range(start, stop):
        tiles[number] = tuple(pltpu.roll(x, number * 29 % LANES, 1) for x in tiles[number])
    sort_tiles(tiles, start, stop)
    end0 = jnp.zeros((8, LANES), F32)
    for number in range(count):
        end0 = jnp.where(tiles[number][1] > 0, float(number + 1), end0)
    begin1 = jnp.full((8, LANES), float(count), F32)
    for number in range(count - 1, -1, -1):
        begin1 = jnp.where(tiles[number][1] < 0, float(number), begin1)
    for number in range(count):
        value, code = tiles[number]
        place = jnp.abs(code)
        high = jnp.floor((place - 1.0) * (1.0 / LOW))
        low = place - high * float(LOW)
        sorted_ref[0, number] = jnp.where(code > 0, value, 0.0).astype(BF16)
        sorted_ref[1, number] = jnp.where(code > 0, 0.0, value).astype(BF16)
        sorted_ref[2, number] = high.astype(BF16)
        sorted_ref[3, number] = low.astype(BF16)

    def one_unit(t, number, carry):
        for step in range(unit):
            value, high, low = (sorted_ref[plane, number * unit + step] for plane in (t, 2, 3))
            left, right = [], []
            for row in range(8):
                left.append(jnp.where(places_hi == high[row : row + 1, :], value[row : row + 1, :], zero))
                right.append(jnp.where(places_lo == low[row : row + 1, :], one, zero))
            acc_ref[t] += dot(jnp.concatenate(left, axis=1), jnp.concatenate(right, axis=1), 1, 1)
        return carry

    end0 = lax.div(jnp.max(end0).astype(jnp.int32) + (unit - 1), unit)
    begin1 = lax.div(jnp.min(begin1).astype(jnp.int32), unit)
    lax.fori_loop(0, end0, lambda number, carry: one_unit(0, number, carry), 0)
    lax.fori_loop(begin1, count // unit, lambda number, carry: one_unit(1, number, carry), 0)
    first_copy.wait()
    first = first_vmem[...]
    mixed = [dot(first, acc_ref[t].astype(BF16), 1, 0).astype(BF16) for t in range(CYCLE_DEV)]
    copy.wait()
    for parity in range(2):
        total = None
        for a0 in range(HALF):
            base = (parity * HALF + a0) * NPSI
            left = jnp.concatenate([part[base : base + NPSI] for part in mixed], axis=0)
            term = dot(left, table_ref[parity, a0 * LOW : (a0 + 1) * LOW, :], 1, 0)
            total = term if total is None else total + term
        total = total.astype(BF16)
        for group in range(groups):
            for beam in range(NPSI // share):
                for t in range(CYCLE_DEV):
                    base = t * NPSI + beam * share
                    out_ref[group, beam, parity, t] = total[
                        base : base + share, group * width : (group + 1) * width
                    ]
    for one in held:
        one.wait()


def coeff_kernel(groups, orders, recv_ref, out_ref):
    _, beams, _, cycles, share, width = recv_ref.shape
    thetas = groups * cycles
    depth = thetas * share
    row = lax.broadcasted_iota(jnp.int32, (depth, depth), 0)
    column = lax.broadcasted_iota(jnp.int32, (depth, depth), 1)
    swap = ((row % share) * thetas + row // share == column).astype(F32).astype(BF16)
    total = None
    for parity in range(2):
        parts = []
        for group in range(groups):
            for t in range(cycles):
                piece = recv_ref[group, 0, parity, t].astype(F32)
                for beam in range(1, beams):
                    piece = piece + recv_ref[group, beam, parity, t].astype(F32)
                parts.append(piece)
        stacked = jnp.concatenate(parts, axis=0).astype(BF16)
        turned = dot(stacked, swap, 0, 0).astype(BF16)
        row = lax.broadcasted_iota(jnp.int32, (2 * orders, width), 0)
        column = lax.broadcasted_iota(jnp.int32, (2 * orders, width), 1)
        place = (row // 4 * 2 + row % 2 == column) & (row // 2 % 2 == parity)
        term = dot(place.astype(F32).astype(BF16), turned, 1, 0)
        total = term if total is None else total + term
    out_ref[...] = total.astype(BF16)


def order_kernel(chunk, offset, late, where_ref, coeff_ref, wigner_ref, *refs):
    depth = coeff_ref.shape[1]
    size = chunk * depth
    copies = []
    if late:
        source_ref, out_ref, late_ref, sem = refs
        first = where_ref[offset] * (out_ref.shape[0] // 2 * depth) + wigner_ref.shape[0]
        for number in range(late):
            source = source_ref.at[pl.ds(first + number * size, size), :]
            copies.append(pltpu.make_async_copy(source, late_ref.at[number], sem.at[number]))
            copies[-1].start()
    else:
        (out_ref,) = refs
    rows = out_ref.shape[0]
    base = where_ref[offset] * rows
    shape = (2 * chunk, size)
    own = lax.broadcasted_iota(jnp.int32, shape, 0) // 2 == lax.broadcasted_iota(jnp.int32, shape, 1) // depth
    early = wigner_ref.shape[0] // size
    for number in range(early + late):
        start = pl.multiple_of(base + number * 2 * chunk, 2 * chunk)
        coeff = coeff_ref[pl.ds(start, 2 * chunk), :].astype(F32)
        wide = jnp.where(own, jnp.concatenate([coeff] * chunk, axis=1), 0.0).astype(BF16)
        if number < early:
            table = wigner_ref[number * size : (number + 1) * size, :]
        else:
            copies[number - early].wait()
            table = late_ref[number - early]
        part = dot(wide, table, 1, 0)
        out_ref[number * 2 * chunk : (number + 1) * 2 * chunk, :] = part.astype(out_ref.dtype)


def first_order_kernel(groups, orders, chunk, offset, where_ref, recv_ref, wigner_ref, coeff_ref, out_ref):
    coeff_kernel(groups, orders, recv_ref, coeff_ref)
    order_kernel(chunk, offset, 0, where_ref, coeff_ref, wigner_ref, out_ref)


def sum_kernel(*refs):
    *terms, out_ref = refs
    total = terms[0][...].astype(F32)
    for term in terms[1:]:
        total = total + term[...].astype(F32)
    out_ref[...] = total.reshape(out_ref.shape)


def shards(signal, weight, cycle, phi, psi, owner, wigner):
    groups = lax.axis_size("blk")
    beams = lax.axis_size("beam")
    blocks = owner.shape[0]
    cap = max(2, 5 * blocks // (2 * groups))
    padded = round_up(cap, 8)
    share = NPSI // beams
    orders = wigner.shape[0]
    ells = wigner.shape[3]
    depth = share * groups * CYCLE_DEV

    def square(data):
        return pltpu.with_memory_space_constraint(data.reshape(blocks, BLOCK_ROWS), pltpu.HBM)

    whole = pl.BlockSpec(memory_space=pltpu.VMEM)
    scalars = pl.BlockSpec(memory_space=pltpu.SMEM)
    anywhere = pl.BlockSpec(memory_space=pl.ANY)
    me = lax.axis_index("beam").astype(jnp.int32)
    shape = (blocks, BLOCK_ROWS)
    sent, targets = pl.pallas_call(
        lambda *refs: pack_kernel(groups, *refs),
        out_shape=(
            jax.ShapeDtypeStruct((groups, 3, padded, BLOCK_ROWS), BF16),
            jax.ShapeDtypeStruct((beams,), jnp.int32),
        ),
        in_specs=[scalars] + [anywhere] * 6,
        out_specs=(whole, scalars),
        scratch_shapes=[pltpu.VMEM((1, blocks), jnp.int32)]
        + [pltpu.VMEM(shape, F32)] * 2
        + [pltpu.VMEM(shape, jnp.int32)] * 3
        + [pltpu.SemaphoreType.DMA((6,))],
        compiler_params=pltpu.CompilerParams(vmem_limit_bytes=6 << 20),
        cost_estimate=pl.CostEstimate(flops=10**11, transcendentals=0, bytes_accessed=10**8),
        name="pack",
    )(
        me.reshape(1),
        pltpu.with_memory_space_constraint(owner.reshape(1, blocks), pltpu.HBM),
        square(signal),
        square(weight),
        square(cycle),
        square(phi),
        square(psi),
    )
    got = lax.all_to_all(sent, "blk", split_axis=0, concat_axis=0, tiled=True)
    tables, width = second_tables(groups)
    tiles = groups * padded // 8
    unit = next(size for size in (5, 4, 2, 1) if tiles % size == 0)
    flat = wigner.reshape(orders * depth, ells)
    mine = orders // beams
    chunk = 8
    steps = mine // chunk
    early = (steps + 1) // 2
    spectra, *held = pl.pallas_call(
        lambda *refs: bin_kernel(share, unit, *refs),
        out_shape=(
            jax.ShapeDtypeStruct((groups, beams, 2, CYCLE_DEV, share, width), BF16),
        )
        + tuple(pltpu.VMEM((count * chunk * depth, ells), BF16) for count in [early] + [steps] * (beams - 1)),
        in_specs=[scalars, whole, anywhere, anywhere, anywhere],
        out_specs=(whole,) * (1 + beams),
        scratch_shapes=[
            pltpu.VMEM((4, tiles, 8, LANES), BF16),
            pltpu.VMEM((CYCLE_DEV, LOW, LOW), F32),
            pltpu.VMEM((LOW, LOW), BF16),
            pltpu.VMEM(tables.shape, BF16),
            pltpu.SemaphoreType.DMA,
            pltpu.SemaphoreType.DMA,
            pltpu.SemaphoreType.DMA((beams,)),
        ],
        compiler_params=pltpu.CompilerParams(vmem_limit_bytes=2 * tables.size + (4 << 20)),
        name="bin",
    )(
        targets,
        got,
        pltpu.with_memory_space_constraint(jnp.asarray(first_matrix(), BF16), pltpu.HBM),
        jnp.asarray(tables, BF16),
        pltpu.with_memory_space_constraint(flat, pltpu.HBM),
    )
    rows = 2 * CYCLE_DEV * share
    spectra = spectra.reshape(groups * beams, rows, width)
    parts = lax.all_to_all(spectra, ("blk", "beam"), split_axis=0, concat_axis=0, tiled=True)
    parts = parts.reshape(groups, beams, 2, CYCLE_DEV, share, width)

    def first_piece(offset, kind):
        return pl.pallas_call(
            lambda *refs: first_order_kernel(groups, orders, chunk, offset, *refs),
            out_shape=(
                jax.ShapeDtypeStruct((2 * orders, depth), BF16),
                jax.ShapeDtypeStruct((2 * mine, ells), kind),
            ),
            in_specs=[scalars, whole, whole],
            out_specs=(whole, whole),
            compiler_params=pltpu.CompilerParams(vmem_limit_bytes=6 << 20),
            name="first",
        )(targets, parts, pltpu.with_memory_space_constraint(held[offset], pltpu.VMEM))

    def piece(coeff, offset, kind):
        late = 0 if offset else steps - early
        table = pltpu.with_memory_space_constraint(held[offset], pltpu.VMEM)
        source = [pltpu.with_memory_space_constraint(flat, pltpu.HBM)] if late else []
        scratch = [pltpu.VMEM((late, chunk * depth, ells), BF16), pltpu.SemaphoreType.DMA((late,))] if late else []
        return pl.pallas_call(
            lambda *refs: order_kernel(chunk, offset, late, *refs),
            out_shape=jax.ShapeDtypeStruct((2 * mine, ells), kind),
            in_specs=[scalars, whole, whole] + [anywhere] * len(source),
            out_specs=whole,
            scratch_shapes=scratch,
            compiler_params=pltpu.CompilerParams(vmem_limit_bytes=6 << 20),
            name="order",
        )(targets, coeff, table, *source)

    def send(part, distance):
        return lax.ppermute(part, "beam", [(i, i ^ distance) for i in range(beams)])

    sequence = [offset for chip in range(beams // 2 - 1, -1, -1) for offset in (2 * chip + 1, 2 * chip)]
    terms = []
    near = None
    for offset in sequence:
        if offset == beams - 1:
            coeff, part = first_piece(offset, BF16)
        else:
            part = piece(coeff, offset, BF16 if offset % 2 else F32)
        if offset % 2:
            near = send(part, 1)
        elif offset:
            terms.append(send((part + near.astype(F32)).astype(BF16), offset))
        else:
            terms = [part, near] + terms
    return pl.pallas_call(
        sum_kernel,
        out_shape=jax.ShapeDtypeStruct((mine, 2, ells), F32),
        compiler_params=pltpu.CompilerParams(vmem_limit_bytes=6 << 20),
        name="sum",
    )(*terms)


def solution(mesh):
    return jax.shard_map(
        shards,
        mesh=mesh,
        in_specs=(
            P(("blk", "beam")),
            P(("blk", "beam")),
            P(("blk", "beam")),
            P(("blk", "beam")),
            P(("blk", "beam")),
            P(("blk", "beam"), None),
            P("blk", "beam", None, None),
        ),
        out_specs=P(("blk", "beam"), None, None),
        check_vma=False,
    )
```

```python
import math

import jax
import jax.numpy as jnp
import numpy as np
from jax import lax
from jax.experimental import pallas as pl
from jax.experimental.pallas import tpu as pltpu
from jax.sharding import PartitionSpec as P


BLOCK_ROWS = 128
CYCLE_DEV = 2
NPSI = 32
NPHI = 2048
LOW = 256
HIGH = NPHI // LOW
HALF = HIGH // 2
LANES = 128
F32 = jnp.float32
BF16 = jnp.bfloat16


def round_up(value, step):
    return -(-value // step) * step


def psi_matrix():
    component = np.arange(NPSI)[:, None]
    cell = np.arange(NPSI)[None, :]
    middle = NPSI // 2
    frequency = np.where(component <= middle, component, component - middle)
    angles = (frequency * cell % NPSI) * (2.0 * math.pi / NPSI)
    return np.where(component <= middle, np.cos(angles), np.sin(angles)) / math.sqrt(NPSI)


def first_matrix():
    psi = psi_matrix()
    out = np.zeros((2, HALF, NPSI, NPSI, HIGH))
    for parity in range(2):
        for a in range(HIGH):
            sign = -1.0 if parity == 1 and a >= HALF else 1.0
            out[parity, a % HALF, :, :, a] = sign * psi
    return out.reshape(2 * HALF * NPSI, NPSI * HIGH)


def second_tables(groups):
    orders = NPHI // 2 // groups
    width = round_up(orders, LANES)
    f = np.arange(NPHI // 2)
    out = np.zeros((2, NPHI // 2, groups, width))
    for parity in range(2):
        k = np.arange(orders // 2)
        m = np.arange(groups)[:, None] * orders + 2 * k[None, :] + parity
        angles = (f[:, None, None] * m[None] % NPHI) * (2.0 * math.pi / NPHI)
        out[parity, :, :, 0:orders:2] = np.cos(angles)
        out[parity, :, :, 1:orders:2] = np.sin(angles)
    out = out / math.sqrt(NPHI)
    return out.reshape(2, NPHI // 2, groups * width), width


def dot(a, b, ca, cb):
    return lax.dot_general(a, b, (((ca,), (cb,)), ((), ())), preferred_element_type=F32)


def pack_kernel(groups, me_ref, *refs):
    sources, (out_ref, targets_ref), held, sems = refs[:6], refs[6:8], refs[8:14], refs[14]
    copies = [
        pltpu.make_async_copy(source, place, sems.at[number])
        for number, (source, place) in enumerate(zip(sources, held))
    ]
    for copy in copies:
        copy.start()
    owner_ref, signal_ref, weight_ref, cycle_ref, phi_ref, psi_ref = held
    copies[0].wait()
    for offset in range(targets_ref.shape[0]):
        targets_ref[offset] = me_ref[0] ^ offset
    blocks = owner_ref.shape[1]
    padded = out_ref.shape[2]
    owner = owner_ref[...]
    rows = round_up(groups, 8)
    hits = (owner == lax.broadcasted_iota(jnp.int32, (rows, blocks), 0)).astype(F32)
    before = (
        lax.broadcasted_iota(jnp.int32, (blocks, blocks), 0)
        < lax.broadcasted_iota(jnp.int32, (blocks, blocks), 1)
    ).astype(F32)
    earlier = dot(hits.astype(BF16), before.astype(BF16), 1, 0)
    within = jnp.sum(earlier * hits, axis=0, keepdims=True)
    position = owner * padded + within.astype(jnp.int32)
    spread = (
        (position == lax.broadcasted_iota(jnp.int32, (groups * padded, blocks), 0))
        .astype(F32)
        .astype(BF16)
    )
    for copy in copies[1:]:
        copy.wait()
    value = (signal_ref[...] * weight_ref[...]).astype(BF16)
    phi = phi_ref[...]
    high = (psi_ref[...] * HIGH + phi // LOW).astype(F32).astype(BF16)
    low = phi % LOW + 1
    low = jnp.where(cycle_ref[...] == 0, low, -low).astype(F32).astype(BF16)
    for number, plane in enumerate((value, high, low)):
        moved = dot(spread, plane, 1, 0).astype(BF16)
        for group in range(groups):
            out_ref[group, number] = moved[group * padded : (group + 1) * padded]


def network(count):
    size = 1
    while size < count:
        size *= 2
    pairs = []
    run = 1
    while run < size:
        gap = run
        while gap >= 1:
            for base in range(gap % run, size - gap, 2 * gap):
                for i in range(base, min(base + gap, size - gap)):
                    if i // (2 * run) == (i + gap) // (2 * run) and i + gap < count:
                        pairs.append((i, i + gap))
            gap //= 2
        run *= 2
    return pairs


def sort_tiles(tiles, first, last):
    for i, j in network(last - first):
        i, j = i + first, j + first
        (value0, code0), (value1, code1) = tiles[i], tiles[j]
        swap = code0 < code1
        tiles[i] = (jnp.where(swap, value1, value0), jnp.maximum(code0, code1))
        tiles[j] = (jnp.where(swap, value0, value1), jnp.minimum(code0, code1))


def bin_kernel(share, unit, targets_ref, recv_ref, first_ref, second_ref, wigner_ref, out_ref, *rest):
    *held_refs, sorted_ref, acc_ref, first_vmem, table_ref, first_sem, sem, held_sem = rest
    first_copy = pltpu.make_async_copy(first_ref, first_vmem, first_sem)
    first_copy.start()
    groups, _, padded, _ = recv_ref.shape
    width = out_ref.shape[-1]
    copy = pltpu.make_async_copy(second_ref, table_ref, sem)
    copy.start()
    held = []
    size = wigner_ref.shape[0] // len(held_refs)
    for number, held_ref in enumerate(held_refs):
        source = wigner_ref.at[pl.ds(targets_ref[number] * size, held_ref.shape[0]), :]
        held.append(pltpu.make_async_copy(source, held_ref, held_sem.at[number]))
        held[-1].start()
    acc_ref[...] = jnp.zeros_like(acc_ref)
    places = lax.broadcasted_iota(jnp.int32, (LOW, LANES), 0).astype(F32)
    places_hi = places.astype(BF16)
    places_lo = (places + 1.0).astype(BF16)
    zero = jnp.zeros((LOW, LANES), BF16)
    one = jnp.ones((LOW, LANES), BF16)

    tiles = []
    for source in range(groups):
        for start in range(0, padded, 8):
            value, high, low = (recv_ref[source, plane, start : start + 8, :].astype(F32) for plane in range(3))
            tiles.append((value, low + jnp.where(low > 0, high, -high) * float(LOW)))
    count = len(tiles)
    sort_tiles(tiles, 0, count)
    start, stop = count // 5, count - count // 5
    for number in range(start, stop):
        tiles[number] = tuple(pltpu.roll(x, number * 29 % LANES, 1) for x in tiles[number])
    sort_tiles(tiles, start, stop)
    end0 = jnp.zeros((8, LANES), F32)
    for number in range(count):
        end0 = jnp.where(tiles[number][1] > 0, float(number + 1), end0)
    begin1 = jnp.full((8, LANES), float(count), F32)
    for number in range(count - 1, -1, -1):
        begin1 = jnp.where(tiles[number][1] < 0, float(number), begin1)
    for number in range(count):
        value, code = tiles[number]
        place = jnp.abs(code)
        high = jnp.floor((place - 1.0) * (1.0 / LOW))
        low = place - high * float(LOW)
        sorted_ref[0, number] = jnp.where(code > 0, value, 0.0).astype(BF16)
        sorted_ref[1, number] = jnp.where(code > 0, 0.0, value).astype(BF16)
        sorted_ref[2, number] = high.astype(BF16)
        sorted_ref[3, number] = low.astype(BF16)

    def one_unit(t, number, carry):
        for step in range(unit):
            value, high, low = (sorted_ref[plane, number * unit + step] for plane in (t, 2, 3))
            left, right = [], []
            for row in range(8):
                left.append(jnp.where(places_hi == high[row : row + 1, :], value[row : row + 1, :], zero))
                right.append(jnp.where(places_lo == low[row : row + 1, :], one, zero))
            acc_ref[t] += dot(jnp.concatenate(left, axis=1), jnp.concatenate(right, axis=1), 1, 1)
        return carry

    end0 = lax.div(jnp.max(end0).astype(jnp.int32) + (unit - 1), unit)
    begin1 = lax.div(jnp.min(begin1).astype(jnp.int32), unit)
    both = jnp.minimum(end0, count // unit - begin1)

    def two_units(number, carry):
        one_unit(0, number, 0)
        return one_unit(1, begin1 + number, carry)

    lax.fori_loop(0, both, two_units, 0)
    lax.fori_loop(both, end0, lambda number, carry: one_unit(0, number, carry), 0)
    lax.fori_loop(begin1 + both, count // unit, lambda number, carry: one_unit(1, number, carry), 0)
    first_copy.wait()
    first = first_vmem[...]
    mixed = [dot(first, acc_ref[t].astype(BF16), 1, 0).astype(BF16) for t in range(CYCLE_DEV)]
    copy.wait()
    for parity in range(2):
        total = None
        for a0 in range(HALF):
            base = (parity * HALF + a0) * NPSI
            left = jnp.concatenate([part[base : base + NPSI] for part in mixed], axis=0)
            term = dot(left, table_ref[parity, a0 * LOW : (a0 + 1) * LOW, :], 1, 0)
            total = term if total is None else total + term
        total = total.astype(BF16)
        for group in range(groups):
            for beam in range(NPSI // share):
                for t in range(CYCLE_DEV):
                    base = t * NPSI + beam * share
                    out_ref[group, beam, parity, t] = total[
                        base : base + share, group * width : (group + 1) * width
                    ]
    for one in held:
        one.wait()


def coeff_kernel(groups, orders, recv_ref, out_ref):
    _, beams, _, cycles, share, width = recv_ref.shape
    thetas = groups * cycles
    depth = thetas * share
    row = lax.broadcasted_iota(jnp.int32, (depth, depth), 0)
    column = lax.broadcasted_iota(jnp.int32, (depth, depth), 1)
    swap = ((row % share) * thetas + row // share == column).astype(F32).astype(BF16)
    total = None
    for parity in range(2):
        parts = []
        for group in range(groups):
            for t in range(cycles):
                piece = recv_ref[group, 0, parity, t].astype(F32)
                for beam in range(1, beams):
                    piece = piece + recv_ref[group, beam, parity, t].astype(F32)
                parts.append(piece)
        stacked = jnp.concatenate(parts, axis=0).astype(BF16)
        turned = dot(stacked, swap, 0, 0).astype(BF16)
        row = lax.broadcasted_iota(jnp.int32, (2 * orders, width), 0)
        column = lax.broadcasted_iota(jnp.int32, (2 * orders, width), 1)
        place = (row // 4 * 2 + row % 2 == column) & (row // 2 % 2 == parity)
        term = dot(place.astype(F32).astype(BF16), turned, 1, 0)
        total = term if total is None else total + term
    out_ref[...] = total.astype(BF16)


def order_kernel(chunk, offset, tables, late, where_ref, coeff_ref, *refs):
    depth = coeff_ref.shape[1]
    size = chunk * depth
    places = [(ref, at) for ref in refs[:tables] for at in range(0, ref.shape[0], size)]
    early = len(places)
    refs = refs[tables:]
    copies = []
    if late:
        source_ref, out_ref, late_ref, sem = refs
        first = where_ref[offset] * (out_ref.shape[0] // 2 * depth) + early * size
        for number in range(late):
            source = source_ref.at[pl.ds(first + number * size, size), :]
            copies.append(pltpu.make_async_copy(source, late_ref.at[number], sem.at[number]))
            copies[-1].start()
    else:
        (out_ref,) = refs
    rows = out_ref.shape[0]
    base = where_ref[offset] * rows
    shape = (2 * chunk, size)
    own = lax.broadcasted_iota(jnp.int32, shape, 0) // 2 == lax.broadcasted_iota(jnp.int32, shape, 1) // depth
    for number in range(early + late):
        start = pl.multiple_of(base + number * 2 * chunk, 2 * chunk)
        coeff = coeff_ref[pl.ds(start, 2 * chunk), :].astype(F32)
        wide = jnp.where(own, jnp.concatenate([coeff] * chunk, axis=1), 0.0).astype(BF16)
        if number < early:
            ref, at = places[number]
            table = ref[at : at + size, :]
        else:
            copies[number - early].wait()
            table = late_ref[number - early]
        part = dot(wide, table, 1, 0)
        out_ref[number * 2 * chunk : (number + 1) * 2 * chunk, :] = part.astype(out_ref.dtype)


def first_order_kernel(groups, orders, chunk, offset, skip, where_ref, recv_ref, wigner_ref, *refs):
    if skip is None:
        coeff_ref, out_ref = refs
    else:
        source_ref, coeff_ref, out_ref, mid_ref, sem = refs
        size = mid_ref.shape[0]
        first = where_ref[0] * wigner_ref.shape[0] + skip * size
        copy = pltpu.make_async_copy(source_ref.at[pl.ds(first, size), :], mid_ref, sem)
        copy.start()
    coeff_kernel(groups, orders, recv_ref, coeff_ref)
    order_kernel(chunk, offset, 1, 0, where_ref, coeff_ref, wigner_ref, out_ref)
    if skip is not None:
        copy.wait()


def sum_kernel(*refs):
    *terms, out_ref = refs
    total = terms[0][...].astype(F32)
    for term in terms[1:]:
        total = total + term[...].astype(F32)
    out_ref[...] = total.reshape(out_ref.shape)


def shards(signal, weight, cycle, phi, psi, owner, wigner):
    groups = lax.axis_size("blk")
    beams = lax.axis_size("beam")
    blocks = owner.shape[0]
    cap = max(2, 5 * blocks // (2 * groups))
    padded = round_up(cap, 8)
    share = NPSI // beams
    orders = wigner.shape[0]
    ells = wigner.shape[3]
    depth = share * groups * CYCLE_DEV

    def square(data):
        return pltpu.with_memory_space_constraint(data.reshape(blocks, BLOCK_ROWS), pltpu.HBM)

    whole = pl.BlockSpec(memory_space=pltpu.VMEM)
    scalars = pl.BlockSpec(memory_space=pltpu.SMEM)
    anywhere = pl.BlockSpec(memory_space=pl.ANY)
    me = lax.axis_index("beam").astype(jnp.int32)
    shape = (blocks, BLOCK_ROWS)
    sent, targets = pl.pallas_call(
        lambda *refs: pack_kernel(groups, *refs),
        out_shape=(
            jax.ShapeDtypeStruct((groups, 3, padded, BLOCK_ROWS), BF16),
            jax.ShapeDtypeStruct((beams,), jnp.int32),
        ),
        in_specs=[scalars] + [anywhere] * 6,
        out_specs=(whole, scalars),
        scratch_shapes=[pltpu.VMEM((1, blocks), jnp.int32)]
        + [pltpu.VMEM(shape, F32)] * 2
        + [pltpu.VMEM(shape, jnp.int32)] * 3
        + [pltpu.SemaphoreType.DMA((6,))],
        compiler_params=pltpu.CompilerParams(vmem_limit_bytes=6 << 20),
        cost_estimate=pl.CostEstimate(flops=10**11, transcendentals=0, bytes_accessed=10**8),
        name="pack",
    )(
        me.reshape(1),
        pltpu.with_memory_space_constraint(owner.reshape(1, blocks), pltpu.HBM),
        square(signal),
        square(weight),
        square(cycle),
        square(phi),
        square(psi),
    )
    got = lax.all_to_all(sent, "blk", split_axis=0, concat_axis=0, tiled=True)
    tables, width = second_tables(groups)
    tiles = groups * padded // 8
    unit = next(size for size in (5, 4, 2, 1) if tiles % size == 0)
    flat = wigner.reshape(orders * depth, ells)
    mine = orders // beams
    chunk = 8
    steps = mine // chunk
    late = steps // 2
    mid = 1 if steps - late > 1 else 0
    early = steps - late - mid
    spectra, *held = pl.pallas_call(
        lambda *refs: bin_kernel(share, unit, *refs),
        out_shape=(
            jax.ShapeDtypeStruct((groups, beams, 2, CYCLE_DEV, share, width), BF16),
        )
        + tuple(pltpu.VMEM((count * chunk * depth, ells), BF16) for count in [early] + [steps] * (beams - 1)),
        in_specs=[scalars, whole, anywhere, anywhere, anywhere],
        out_specs=(whole,) * (1 + beams),
        scratch_shapes=[
            pltpu.VMEM((4, tiles, 8, LANES), BF16),
            pltpu.VMEM((CYCLE_DEV, LOW, LOW), F32),
            pltpu.VMEM((LOW, LOW), BF16),
            pltpu.VMEM(tables.shape, BF16),
            pltpu.SemaphoreType.DMA,
            pltpu.SemaphoreType.DMA,
            pltpu.SemaphoreType.DMA((beams,)),
        ],
        compiler_params=pltpu.CompilerParams(vmem_limit_bytes=2 * tables.size + (4 << 20)),
        name="bin",
    )(
        targets,
        got,
        pltpu.with_memory_space_constraint(jnp.asarray(first_matrix(), BF16), pltpu.HBM),
        jnp.asarray(tables, BF16),
        pltpu.with_memory_space_constraint(flat, pltpu.HBM),
    )
    rows = 2 * CYCLE_DEV * share
    spectra = spectra.reshape(groups * beams, rows, width)
    parts = lax.all_to_all(spectra, ("blk", "beam"), split_axis=0, concat_axis=0, tiled=True)
    parts = parts.reshape(groups, beams, 2, CYCLE_DEV, share, width)
    distant = pltpu.with_memory_space_constraint(flat, pltpu.HBM)

    def first_piece(offset, kind):
        table = pltpu.with_memory_space_constraint(held[offset], pltpu.VMEM)
        return pl.pallas_call(
            lambda *refs: first_order_kernel(groups, orders, chunk, offset, early if mid else None, *refs),
            out_shape=(
                jax.ShapeDtypeStruct((2 * orders, depth), BF16),
                jax.ShapeDtypeStruct((2 * mine, ells), kind),
            )
            + (pltpu.VMEM((chunk * depth, ells), BF16),) * mid,
            in_specs=[scalars, whole, whole] + [anywhere] * mid,
            out_specs=(whole,) * (2 + mid),
            scratch_shapes=[pltpu.SemaphoreType.DMA] * mid,
            compiler_params=pltpu.CompilerParams(vmem_limit_bytes=6 << 20),
            name="first",
        )(targets, parts, table, *[distant] * mid)

    def piece(coeff, offset, tables, kind):
        tables = [pltpu.with_memory_space_constraint(table, pltpu.VMEM) for table in tables]
        rest = 0 if offset else late
        scratch = [pltpu.VMEM((rest, chunk * depth, ells), BF16), pltpu.SemaphoreType.DMA((rest,))] if rest else []
        return pl.pallas_call(
            lambda *refs: order_kernel(chunk, offset, len(tables), rest, *refs),
            out_shape=jax.ShapeDtypeStruct((2 * mine, ells), kind),
            in_specs=[scalars, whole] + [whole] * len(tables) + [anywhere] * min(rest, 1),
            out_specs=whole,
            scratch_shapes=scratch,
            compiler_params=pltpu.CompilerParams(vmem_limit_bytes=6 << 20),
            name="order",
        )(targets, coeff, *tables, *[distant] * min(rest, 1))

    def send(part, distance):
        return lax.ppermute(part, "beam", [(i, i ^ distance) for i in range(beams)])

    sequence = [offset for chip in range(beams // 2 - 1, -1, -1) for offset in (2 * chip + 1, 2 * chip)]
    terms = []
    near = None
    for offset in sequence:
        if offset == beams - 1:
            coeff, part, *fetched = first_piece(offset, BF16)
        else:
            tables = [held[offset]] + ([] if offset else fetched)
            part = piece(coeff, offset, tables, BF16 if offset % 2 else F32)
        if offset % 2:
            near = send(part, 1)
        elif offset:
            terms.append(send((part + near.astype(F32)).astype(BF16), offset))
        else:
            terms = [part, near] + terms
    return pl.pallas_call(
        sum_kernel,
        out_shape=jax.ShapeDtypeStruct((mine, 2, ells), F32),
        compiler_params=pltpu.CompilerParams(vmem_limit_bytes=6 << 20),
        name="sum",
    )(*terms)


def solution(mesh):
    return jax.shard_map(
        shards,
        mesh=mesh,
        in_specs=(
            P(("blk", "beam")),
            P(("blk", "beam")),
            P(("blk", "beam")),
            P(("blk", "beam")),
            P(("blk", "beam")),
            P(("blk", "beam"), None),
            P("blk", "beam", None, None),
        ),
        out_specs=P(("blk", "beam"), None, None),
        check_vma=False,
    )
```

```python
import math

import jax
import jax.numpy as jnp
import numpy as np
from jax import lax
from jax.experimental import pallas as pl
from jax.experimental.pallas import tpu as pltpu
from jax.sharding import PartitionSpec as P


BLOCK_ROWS = 128
CYCLE_DEV = 2
NPSI = 32
NPHI = 2048
LOW = 256
HIGH = NPHI // LOW
HALF = HIGH // 2
LANES = 128
F32 = jnp.float32
BF16 = jnp.bfloat16


def round_up(value, step):
    return -(-value // step) * step


def psi_matrix():
    component = np.arange(NPSI)[:, None]
    cell = np.arange(NPSI)[None, :]
    middle = NPSI // 2
    frequency = np.where(component <= middle, component, component - middle)
    angles = (frequency * cell % NPSI) * (2.0 * math.pi / NPSI)
    return np.where(component <= middle, np.cos(angles), np.sin(angles)) / math.sqrt(NPSI)


def first_matrix():
    psi = psi_matrix()
    out = np.zeros((2, HALF, NPSI, NPSI, HIGH))
    for parity in range(2):
        for a in range(HIGH):
            sign = -1.0 if parity == 1 and a >= HALF else 1.0
            out[parity, a % HALF, :, :, a] = sign * psi
    return out.reshape(2 * HALF * NPSI, NPSI * HIGH)


def second_tables(groups):
    orders = NPHI // 2 // groups
    width = round_up(orders, LANES)
    f = np.arange(NPHI // 2)
    out = np.zeros((2, NPHI // 2, groups, width))
    for parity in range(2):
        k = np.arange(orders // 2)
        m = np.arange(groups)[:, None] * orders + 2 * k[None, :] + parity
        angles = (f[:, None, None] * m[None] % NPHI) * (2.0 * math.pi / NPHI)
        out[parity, :, :, 0:orders:2] = np.cos(angles)
        out[parity, :, :, 1:orders:2] = np.sin(angles)
    out = out / math.sqrt(NPHI)
    return out.reshape(2, NPHI // 2, groups * width), width


def dot(a, b, ca, cb):
    return lax.dot_general(a, b, (((ca,), (cb,)), ((), ())), preferred_element_type=F32)


def pack_kernel(groups, me_ref, *refs):
    sources, (out_ref, targets_ref), held, sems = refs[:6], refs[6:8], refs[8:14], refs[14]
    copies = [
        pltpu.make_async_copy(source, place, sems.at[number])
        for number, (source, place) in enumerate(zip(sources, held))
    ]
    for copy in copies:
        copy.start()
    owner_ref, signal_ref, weight_ref, cycle_ref, phi_ref, psi_ref = held
    copies[0].wait()
    for offset in range(targets_ref.shape[0]):
        targets_ref[offset] = me_ref[0] ^ offset
    blocks = owner_ref.shape[1]
    padded = out_ref.shape[2]
    owner = owner_ref[...]
    rows = round_up(groups, 8)
    hits = (owner == lax.broadcasted_iota(jnp.int32, (rows, blocks), 0)).astype(F32)
    before = (
        lax.broadcasted_iota(jnp.int32, (blocks, blocks), 0)
        < lax.broadcasted_iota(jnp.int32, (blocks, blocks), 1)
    ).astype(F32)
    earlier = dot(hits.astype(BF16), before.astype(BF16), 1, 0)
    within = jnp.sum(earlier * hits, axis=0, keepdims=True)
    position = owner * padded + within.astype(jnp.int32)
    spread = (
        (position == lax.broadcasted_iota(jnp.int32, (groups * padded, blocks), 0))
        .astype(F32)
        .astype(BF16)
    )
    for copy in copies[1:]:
        copy.wait()
    value = (signal_ref[...] * weight_ref[...]).astype(BF16)
    phi = phi_ref[...]
    high = (psi_ref[...] * HIGH + phi // LOW).astype(F32).astype(BF16)
    low = phi % LOW + 1
    low = jnp.where(cycle_ref[...] == 0, low, -low).astype(F32).astype(BF16)
    for number, plane in enumerate((value, high, low)):
        moved = dot(spread, plane, 1, 0).astype(BF16)
        for group in range(groups):
            out_ref[group, number] = moved[group * padded : (group + 1) * padded]


def network(count):
    size = 1
    while size < count:
        size *= 2
    pairs = []
    run = 1
    while run < size:
        gap = run
        while gap >= 1:
            for base in range(gap % run, size - gap, 2 * gap):
                for i in range(base, min(base + gap, size - gap)):
                    if i // (2 * run) == (i + gap) // (2 * run) and i + gap < count:
                        pairs.append((i, i + gap))
            gap //= 2
        run *= 2
    return pairs


def sort_tiles(tiles, first, last):
    for i, j in network(last - first):
        i, j = i + first, j + first
        (value0, code0), (value1, code1) = tiles[i], tiles[j]
        swap = code0 < code1
        tiles[i] = (jnp.where(swap, value1, value0), jnp.maximum(code0, code1))
        tiles[j] = (jnp.where(swap, value0, value1), jnp.minimum(code0, code1))


def bin_kernel(share, unit, targets_ref, recv_ref, first_ref, second_ref, wigner_ref, out_ref, *rest):
    *held_refs, sorted_ref, acc_ref, first_vmem, table_ref, first_sem, sem, held_sem = rest
    first_copy = pltpu.make_async_copy(first_ref, first_vmem, first_sem)
    first_copy.start()
    groups, _, padded, _ = recv_ref.shape
    width = out_ref.shape[-1]
    copy = pltpu.make_async_copy(second_ref, table_ref, sem)
    copy.start()
    held = []
    size = wigner_ref.shape[0] // len(held_refs)
    for number, held_ref in enumerate(held_refs):
        source = wigner_ref.at[pl.ds(targets_ref[number] * size, held_ref.shape[0]), :]
        held.append(pltpu.make_async_copy(source, held_ref, held_sem.at[number]))
        held[-1].start()
    acc_ref[...] = jnp.zeros_like(acc_ref)
    places = lax.broadcasted_iota(jnp.int32, (LOW, LANES), 0).astype(F32)
    places_hi = places.astype(BF16)
    places_lo = (places + 1.0).astype(BF16)
    zero = jnp.zeros((LOW, LANES), BF16)
    one = jnp.ones((LOW, LANES), BF16)

    tiles = []
    for source in range(groups):
        for start in range(0, padded, 8):
            value, high, low = (recv_ref[source, plane, start : start + 8, :].astype(F32) for plane in range(3))
            tiles.append((value, low + jnp.where(low > 0, high, -high) * float(LOW)))
    count = len(tiles)
    sort_tiles(tiles, 0, count)
    start, stop = count // 5, count - count // 5
    for number in range(start, stop):
        tiles[number] = tuple(pltpu.roll(x, number * 29 % LANES, 1) for x in tiles[number])
    sort_tiles(tiles, start, stop)
    end0 = jnp.zeros((8, LANES), F32)
    for number in range(count):
        end0 = jnp.where(tiles[number][1] > 0, float(number + 1), end0)
    begin1 = jnp.full((8, LANES), float(count), F32)
    for number in range(count - 1, -1, -1):
        begin1 = jnp.where(tiles[number][1] < 0, float(number), begin1)
    for number in range(count):
        value, code = tiles[number]
        place = jnp.abs(code)
        high = jnp.floor((place - 1.0) * (1.0 / LOW))
        low = place - high * float(LOW)
        sorted_ref[0, number] = jnp.where(code > 0, value, 0.0).astype(BF16)
        sorted_ref[1, number] = jnp.where(code > 0, 0.0, value).astype(BF16)
        sorted_ref[2, number] = high.astype(BF16)
        sorted_ref[3, number] = low.astype(BF16)

    def one_unit(t, number, carry):
        for step in range(unit):
            value, high, low = (sorted_ref[plane, number * unit + step] for plane in (t, 2, 3))
            left, right = [], []
            for row in range(8):
                left.append(jnp.where(places_hi == high[row : row + 1, :], value[row : row + 1, :], zero))
                right.append(jnp.where(places_lo == low[row : row + 1, :], one, zero))
            acc_ref[t] += dot(jnp.concatenate(left, axis=1), jnp.concatenate(right, axis=1), 1, 1)
        return carry

    end0 = lax.div(jnp.max(end0).astype(jnp.int32) + (unit - 1), unit)
    begin1 = lax.div(jnp.min(begin1).astype(jnp.int32), unit)
    both = jnp.minimum(end0, count // unit - begin1)

    def two_units(number, carry):
        one_unit(0, number, 0)
        return one_unit(1, begin1 + number, carry)

    lax.fori_loop(0, both, two_units, 0)
    lax.fori_loop(both, end0, lambda number, carry: one_unit(0, number, carry), 0)
    lax.fori_loop(begin1 + both, count // unit, lambda number, carry: one_unit(1, number, carry), 0)
    first_copy.wait()
    first = first_vmem[...]
    mixed = [dot(first, acc_ref[t].astype(BF16), 1, 0).astype(BF16) for t in range(CYCLE_DEV)]
    copy.wait()
    for parity in range(2):
        total = None
        for a0 in range(HALF):
            base = (parity * HALF + a0) * NPSI
            left = jnp.concatenate([part[base : base + NPSI] for part in mixed], axis=0)
            term = dot(left, table_ref[parity, a0 * LOW : (a0 + 1) * LOW, :], 1, 0)
            total = term if total is None else total + term
        total = total.astype(BF16)
        for group in range(groups):
            for beam in range(NPSI // share):
                for t in range(CYCLE_DEV):
                    base = t * NPSI + beam * share
                    out_ref[group, beam, parity, t] = total[
                        base : base + share, group * width : (group + 1) * width
                    ]
    for one in held:
        one.wait()


def coeff_kernel(groups, orders, recv_ref, out_ref):
    _, beams, _, cycles, share, width = recv_ref.shape
    thetas = groups * cycles
    depth = thetas * share
    row = lax.broadcasted_iota(jnp.int32, (depth, depth), 0)
    column = lax.broadcasted_iota(jnp.int32, (depth, depth), 1)
    swap = ((row % share) * thetas + row // share == column).astype(F32).astype(BF16)
    total = None
    for parity in range(2):
        parts = []
        for group in range(groups):
            for t in range(cycles):
                piece = recv_ref[group, 0, parity, t].astype(F32)
                for beam in range(1, beams):
                    piece = piece + recv_ref[group, beam, parity, t].astype(F32)
                parts.append(piece)
        stacked = jnp.concatenate(parts, axis=0).astype(BF16)
        turned = dot(stacked, swap, 0, 0).astype(BF16)
        row = lax.broadcasted_iota(jnp.int32, (2 * orders, width), 0)
        column = lax.broadcasted_iota(jnp.int32, (2 * orders, width), 1)
        place = (row // 4 * 2 + row % 2 == column) & (row // 2 % 2 == parity)
        term = dot(place.astype(F32).astype(BF16), turned, 1, 0)
        total = term if total is None else total + term
    out_ref[...] = total.astype(BF16)


def order_kernel(chunk, offset, late, where_ref, coeff_ref, wigner_ref, *refs):
    depth = coeff_ref.shape[1]
    size = chunk * depth
    copies = []
    if late:
        source_ref, out_ref, late_ref, sem = refs
        first = where_ref[offset] * (out_ref.shape[0] // 2 * depth) + wigner_ref.shape[0]
        for number in range(late):
            source = source_ref.at[pl.ds(first + number * size, size), :]
            copies.append(pltpu.make_async_copy(source, late_ref.at[number], sem.at[number]))
            copies[-1].start()
    else:
        (out_ref,) = refs
    rows = out_ref.shape[0]
    base = where_ref[offset] * rows
    shape = (2 * chunk, size)
    own = lax.broadcasted_iota(jnp.int32, shape, 0) // 2 == lax.broadcasted_iota(jnp.int32, shape, 1) // depth
    early = wigner_ref.shape[0] // size
    for number in range(early + late):
        start = pl.multiple_of(base + number * 2 * chunk, 2 * chunk)
        coeff = coeff_ref[pl.ds(start, 2 * chunk), :].astype(F32)
        wide = jnp.where(own, jnp.concatenate([coeff] * chunk, axis=1), 0.0).astype(BF16)
        if number < early:
            table = wigner_ref[number * size : (number + 1) * size, :]
        else:
            copies[number - early].wait()
            table = late_ref[number - early]
        part = dot(wide, table, 1, 0)
        out_ref[number * 2 * chunk : (number + 1) * 2 * chunk, :] = part.astype(out_ref.dtype)


def first_order_kernel(groups, orders, chunk, offset, where_ref, recv_ref, wigner_ref, coeff_ref, out_ref):
    coeff_kernel(groups, orders, recv_ref, coeff_ref)
    order_kernel(chunk, offset, 0, where_ref, coeff_ref, wigner_ref, out_ref)


def sum_kernel(*refs):
    *terms, out_ref = refs
    total = terms[0][...].astype(F32)
    for term in terms[1:]:
        total = total + term[...].astype(F32)
    out_ref[...] = total.reshape(out_ref.shape)


def shards(signal, weight, cycle, phi, psi, owner, wigner):
    groups = lax.axis_size("blk")
    beams = lax.axis_size("beam")
    blocks = owner.shape[0]
    cap = max(2, 5 * blocks // (2 * groups))
    padded = round_up(cap, 8)
    share = NPSI // beams
    orders = wigner.shape[0]
    ells = wigner.shape[3]
    depth = share * groups * CYCLE_DEV

    def square(data):
        return pltpu.with_memory_space_constraint(data.reshape(blocks, BLOCK_ROWS), pltpu.HBM)

    whole = pl.BlockSpec(memory_space=pltpu.VMEM)
    scalars = pl.BlockSpec(memory_space=pltpu.SMEM)
    anywhere = pl.BlockSpec(memory_space=pl.ANY)
    me = lax.axis_index("beam").astype(jnp.int32)
    shape = (blocks, BLOCK_ROWS)
    sent, targets = pl.pallas_call(
        lambda *refs: pack_kernel(groups, *refs),
        out_shape=(
            jax.ShapeDtypeStruct((groups, 3, padded, BLOCK_ROWS), BF16),
            jax.ShapeDtypeStruct((beams,), jnp.int32),
        ),
        in_specs=[scalars] + [anywhere] * 6,
        out_specs=(whole, scalars),
        scratch_shapes=[pltpu.VMEM((1, blocks), jnp.int32)]
        + [pltpu.VMEM(shape, F32)] * 2
        + [pltpu.VMEM(shape, jnp.int32)] * 3
        + [pltpu.SemaphoreType.DMA((6,))],
        compiler_params=pltpu.CompilerParams(vmem_limit_bytes=6 << 20),
        cost_estimate=pl.CostEstimate(flops=10**11, transcendentals=0, bytes_accessed=10**8),
        name="pack",
    )(
        me.reshape(1),
        pltpu.with_memory_space_constraint(owner.reshape(1, blocks), pltpu.HBM),
        square(signal),
        square(weight),
        square(cycle),
        square(phi),
        square(psi),
    )
    got = lax.all_to_all(sent, "blk", split_axis=0, concat_axis=0, tiled=True)
    tables, width = second_tables(groups)
    tiles = groups * padded // 8
    unit = next(size for size in (5, 4, 2, 1) if tiles % size == 0)
    flat = wigner.reshape(orders * depth, ells)
    mine = orders // beams
    chunk = 8
    steps = mine // chunk
    early = (steps + 1) // 2
    spectra, *held = pl.pallas_call(
        lambda *refs: bin_kernel(share, unit, *refs),
        out_shape=(
            jax.ShapeDtypeStruct((groups, beams, 2, CYCLE_DEV, share, width), BF16),
        )
        + tuple(pltpu.VMEM((count * chunk * depth, ells), BF16) for count in [early] + [steps] * (beams - 1)),
        in_specs=[scalars, whole, anywhere, anywhere, anywhere],
        out_specs=(whole,) * (1 + beams),
        scratch_shapes=[
            pltpu.VMEM((4, tiles, 8, LANES), BF16),
            pltpu.VMEM((CYCLE_DEV, LOW, LOW), F32),
            pltpu.VMEM((LOW, LOW), BF16),
            pltpu.VMEM(tables.shape, BF16),
            pltpu.SemaphoreType.DMA,
            pltpu.SemaphoreType.DMA,
            pltpu.SemaphoreType.DMA((beams,)),
        ],
        compiler_params=pltpu.CompilerParams(vmem_limit_bytes=2 * tables.size + (4 << 20)),
        name="bin",
    )(
        targets,
        got,
        pltpu.with_memory_space_constraint(jnp.asarray(first_matrix(), BF16), pltpu.HBM),
        jnp.asarray(tables, BF16),
        pltpu.with_memory_space_constraint(flat, pltpu.HBM),
    )
    rows = 2 * CYCLE_DEV * share
    spectra = spectra.reshape(groups * beams, rows, width)
    parts = lax.all_to_all(spectra, ("blk", "beam"), split_axis=0, concat_axis=0, tiled=True)
    parts = parts.reshape(groups, beams, 2, CYCLE_DEV, share, width)

    def first_piece(offset, kind):
        return pl.pallas_call(
            lambda *refs: first_order_kernel(groups, orders, chunk, offset, *refs),
            out_shape=(
                jax.ShapeDtypeStruct((2 * orders, depth), BF16),
                jax.ShapeDtypeStruct((2 * mine, ells), kind),
            ),
            in_specs=[scalars, whole, whole],
            out_specs=(whole, whole),
            compiler_params=pltpu.CompilerParams(vmem_limit_bytes=6 << 20),
            name="first",
        )(targets, parts, pltpu.with_memory_space_constraint(held[offset], pltpu.VMEM))

    def piece(coeff, offset, kind):
        late = 0 if offset else steps - early
        table = pltpu.with_memory_space_constraint(held[offset], pltpu.VMEM)
        source = [pltpu.with_memory_space_constraint(flat, pltpu.HBM)] if late else []
        scratch = [pltpu.VMEM((late, chunk * depth, ells), BF16), pltpu.SemaphoreType.DMA((late,))] if late else []
        return pl.pallas_call(
            lambda *refs: order_kernel(chunk, offset, late, *refs),
            out_shape=jax.ShapeDtypeStruct((2 * mine, ells), kind),
            in_specs=[scalars, whole, whole] + [anywhere] * len(source),
            out_specs=whole,
            scratch_shapes=scratch,
            compiler_params=pltpu.CompilerParams(vmem_limit_bytes=6 << 20),
            name="order",
        )(targets, coeff, table, *source)

    def send(part, distance):
        return lax.ppermute(part, "beam", [(i, i ^ distance) for i in range(beams)])

    sequence = [offset for chip in range(beams // 2 - 1, -1, -1) for offset in (2 * chip + 1, 2 * chip)]
    terms = []
    near = None
    for offset in sequence:
        if offset == beams - 1:
            coeff, part = first_piece(offset, BF16)
        else:
            part = piece(coeff, offset, BF16 if offset % 2 else F32)
        if offset % 2:
            near = send(part, 1)
        elif offset:
            terms.append(send((part + near.astype(F32)).astype(BF16), offset))
        else:
            terms = [part, near] + terms
    return pl.pallas_call(
        sum_kernel,
        out_shape=jax.ShapeDtypeStruct((mine, 2, ells), F32),
        compiler_params=pltpu.CompilerParams(vmem_limit_bytes=6 << 20),
        name="sum",
    )(*terms)


def solution(mesh):
    return jax.shard_map(
        shards,
        mesh=mesh,
        in_specs=(
            P(("blk", "beam")),
            P(("blk", "beam")),
            P(("blk", "beam")),
            P(("blk", "beam")),
            P(("blk", "beam")),
            P(("blk", "beam"), None),
            P("blk", "beam", None, None),
        ),
        out_specs=P(("blk", "beam"), None, None),
        check_vma=False,
    )
```
